512 devices in a mesh: region: 32 (over x_hi, z), mode: 16 (over y, x_lo, core).
Axes of the slice: x: 4 (x_hi: 2, x_lo: 2; x = x_hi * 2 + x_lo), y: 4, z: 16, core: 2. Of those that a mesh axis runs over, the one named last changes fastest.
Arguments:
- measured: float32 [64, 256, 256], P('region'), may hold values from 0.05 to 20
- probe_modes: float32 [2, 16, 256, 256], P(None, 'mode'), may hold values from -1.5 to 1.5
- object_bands: float32 [2, 4096, 512], P(None, 'region'), may hold values from -4.2 to 4.2
- scan_offsets: int32 [64, 2], replicated, may hold values from 0 to 3839, as said below
- band_owner: int32 [32], replicated, may hold values from 0 to 31, each once
Outputs:
- probe_out: float32 [2, 16, 256, 256], P(None, 'mode')
- object_out: float32 [2, 4096, 512], P(None, 'region')
The draws below stay inside these ranges and needn't reach their ends.
Inputs may be any that keep to these rules, and one draw needn't show every extreme that they name: `scan_offsets`: every frame covers rows r to r + 255 within the bands r // 128 to r // 128 + 2; no band is covered by two frames of one region (frames f * 2 to f * 2 + 1 form region f).
All inputs are finite; a program needn't handle non-finite values.
Results may differ from the reference program's by a relative error of at most 0.0001.
Values sent between devices are 32-bit elements; how exact they have to be, the bound alone decides.
A program may use at most 64 MiB of HBM per device.

```python
import math
import jax
import jax.numpy as jnp
from jax import lax

N = 256
ITERS = 1
OBJ_X = 512
F_DEV = 2
MODES = 16
FRAMES = 64
OBJ_Y = 4096
N_REGION = 32


def draw_scan_offsets(key, part):
    region_keys = jax.random.split(jax.random.fold_in(key, 11), N_REGION)
    spots = N_REGION - 2 * F_DEV

    def one_region(region_key):
        first_key, second_key, third_key, fourth_key = jax.random.split(region_key, 4)
        chosen = jnp.sort(jax.random.permutation(first_key, spots)[:F_DEV])
        anchors = chosen + 2 * jnp.arange(F_DEV, dtype=jnp.int32)
        anchors = jax.random.permutation(fourth_key, anchors)
        lead_rows = jax.random.randint(second_key, (F_DEV,), 0, N // 2)
        columns = jax.random.randint(third_key, (F_DEV,), 0, OBJ_X - N + 1)
        return jnp.stack([anchors * (N // 2) + lead_rows, columns], axis=1)
    return jax.vmap(one_region)(region_keys).reshape(N_REGION * F_DEV, 2).astype(jnp.int32)


def shard_levels(stream_key, dims, pieces, low, largest):
    gain = 1.0
    for position, shards_of in pieces:
        steps = jax.random.uniform(jax.random.fold_in(jax.random.fold_in(stream_key, 6), position), (shards_of,), jnp.float32, low / len(pieces), largest / len(pieces))
        gain = gain * jnp.repeat(jnp.exp(steps), dims[position] // shards_of).reshape((-1,) + (1,) * (len(dims) - 1 - position))
    return gain


def scatter_about(rng, extent, width, limit, cuts=(), kind=jnp.bfloat16):
    gain = shard_levels(rng, extent, cuts, -0.22, 0.18) if cuts else 1.0
    result = jax.random.normal(rng, extent, jnp.float32) * width * gain
    return jnp.minimum(jnp.maximum(result, -limit), limit).astype(kind)


def setup_inputs(seed: int = 0) -> dict:
    splits = jax.random.split(jax.random.key(seed), 6)
    return {
        "measured": jnp.clip(jnp.exp(math.log(20.0) - 5.9914645 * jax.random.uniform(splits[0], (FRAMES, N, N), jnp.float32) ** shard_levels(splits[0], (FRAMES, N, N), ((0, 32),), -0.2, 0.2)), 0.05, 20.0),
        "probe_modes": scatter_about(splits[1], (2, MODES, N, N), 0.25, 1.5, ((1, 16),), jnp.float32),
        "object_bands": scatter_about(splits[2], (2, OBJ_Y, OBJ_X), 0.7, 4.2, ((1, 32),), jnp.float32),
        "scan_offsets": draw_scan_offsets(jax.random.fold_in(splits[5], 71), 0),
        "band_owner": jax.random.permutation(splits[4], N_REGION).astype(jnp.int32),
    }


intensity_offset = 0.1
probe_damping = 1.0
object_damping = 1.0

def to_complex(planes):
    return lax.complex(planes[0], planes[1])

def wave_change(probe_wave, window_wave, measured_frame):
    exit_waves = probe_wave * window_wave[None]
    far_field = jnp.fft.fft2(exit_waves, norm='ortho')
    intensity = lax.optimization_barrier(jnp.sum(jnp.real(far_field) ** 2 + jnp.imag(far_field) ** 2, axis=0))
    factor = jnp.sqrt(measured_frame) / jnp.sqrt(intensity + intensity_offset) - 1.0
    return jnp.fft.ifft2(far_field * factor[None], norm='ortho')

def reference(measured, probe_modes, object_bands, scan_offsets, band_owner):
    band_rows = N // 2
    stored = object_bands.reshape(2, N_REGION, band_rows, OBJ_X)
    ordered = jnp.take(stored, band_owner, axis=1).reshape(2, N_REGION * band_rows, OBJ_X)
    object_image = to_complex(ordered)
    probe_wave = to_complex(probe_modes)

    def window_of(offset):
        return lax.dynamic_slice(object_image, (offset[0], offset[1]), (N, N))

    def add_power(summed, offset):
        window_wave = window_of(offset)
        return (summed + jnp.real(window_wave) ** 2 + jnp.imag(window_wave) ** 2, None)
    object_power, unused = lax.scan(add_power, jnp.zeros((N, N), jnp.float32), scan_offsets)
    for iteration in range(ITERS):

        def add_gradient(summed, inputs):
            offset, measured_frame = inputs
            window_wave = window_of(offset)
            change = wave_change(probe_wave, window_wave, measured_frame)
            return (summed + jnp.conj(window_wave)[None] * change, None)
        gradient, unused = lax.scan(add_gradient, jnp.zeros_like(probe_wave), (scan_offsets, measured))
        probe_wave = probe_wave + gradient / (object_power + probe_damping)
    density_frame = lax.optimization_barrier(jnp.sum(jnp.real(probe_wave) ** 2 + jnp.imag(probe_wave) ** 2, axis=0))

    def add_update(totals, inputs):
        numerator, density = totals
        offset, measured_frame = inputs
        window_wave = window_of(offset)
        change = wave_change(probe_wave, window_wave, measured_frame)
        update_term = lax.optimization_barrier(jnp.sum(jnp.conj(probe_wave) * change, axis=0))
        corner = (offset[0], offset[1])
        numerator = lax.dynamic_update_slice(numerator, lax.dynamic_slice(numerator, corner, (N, N)) + update_term, corner)
        density = lax.dynamic_update_slice(density, lax.dynamic_slice(density, corner, (N, N)) + density_frame, corner)
        return ((numerator, density), None)
    start_totals = (jnp.zeros_like(object_image), jnp.zeros(object_image.shape, jnp.float32))
    (numerator, density), unused = lax.scan(add_update, start_totals, (scan_offsets, measured))
    updated = object_image + numerator / (density + object_damping)
    planes = jnp.stack([jnp.real(updated), jnp.imag(updated)])
    restored = jnp.zeros_like(stored).at[:, band_owner].set(planes.reshape(2, N_REGION, band_rows, OBJ_X))
    probe_planes = jnp.stack([jnp.real(probe_wave), jnp.imag(probe_wave)])
    return (probe_planes, restored.reshape(2, N_REGION * band_rows, OBJ_X))
```

```python
import functools
import math

import jax
import jax.numpy as jnp
import numpy as np
from jax import lax
from jax.experimental import pallas as pl
from jax.experimental.pallas import tpu as pltpu
from jax.sharding import PartitionSpec as P

N = 256
BAND = 128
WIDTH = 512
FRAMES = 64
F_DEV = 2
REGIONS = 32
MODES = 16
Z = 16
Y = 4
SHARE = BAND // MODES
f32 = jnp.float32
bf16 = jnp.bfloat16

VMEM = pl.BlockSpec(memory_space=pltpu.VMEM)
SMEM = pl.BlockSpec(memory_space=pltpu.SMEM)
DMA = pltpu.SemaphoreType.DMA

NEAR = ((2, 1), (2, 0), (1, 1), (3, 1), (1, 0), (3, 0), (0, 1), (0, 0))
OTHERS = len(NEAR) - 1


def send(src, dst, send_sem, recv_sem, axis, index):
    copy = pltpu.make_async_remote_copy(
        src_ref=src,
        dst_ref=dst,
        send_sem=send_sem,
        recv_sem=recv_sem,
        device_id={axis: index},
        device_id_type=pl.DeviceIdType.MESH,
    )
    copy.start()
    return copy


def greet(axis, peers):
    barrier = pltpu.get_barrier_semaphore()
    for peer in peers:
        pl.semaphore_signal(
            barrier, inc=1, device_id={axis: peer}, device_id_type=pl.DeviceIdType.MESH
        )
    pl.semaphore_wait(barrier, len(peers))


class ModeGroup:
    def __init__(self):
        self.me = lax.axis_index("mode")
        self.y = self.me // 4
        self.x = (self.me // 2) % 2
        self.core = self.me % 2
        self.twin = self.me + 1 - 2 * self.core

    def chip(self, dy, dx):
        return ((self.y + dy) % Y) * 2 + (self.x + dx) % 2

    def chip_before(self, dy, dx):
        return ((self.y + Y - dy) % Y) * 2 + (self.x + 2 - dx) % 2

    def peers(self):
        return [2 * self.chip(dy, dx) + self.core for dy, dx in NEAR[:OTHERS]] + [self.twin]


def mode_scatter(group, x_ref, twin_buf, peer_buf, sems):
    twin_send, twin_recv, peer_send, peer_recv = sems
    twin_copies = []
    for i, (dy, dx) in enumerate(NEAR):
        block = 2 * group.chip(dy, dx) + 1 - group.core
        twin_copies.append(
            send(x_ref.at[:, block], twin_buf.at[i], twin_send.at[i], twin_recv.at[i], "mode", group.twin)
        )
    peer_copies = []
    for i, (dy, dx) in enumerate(NEAR):
        target = 2 * group.chip(dy, dx) + group.core
        twin_copies[i].wait_recv()
        twin_buf[i] = twin_buf[i] + x_ref[:, target]
        if i < OTHERS:
            peer_copies.append(
                send(twin_buf.at[i], peer_buf.at[i], peer_send.at[i], peer_recv.at[i], "mode", target)
            )
    total = twin_buf[OTHERS]
    for i in reversed(range(OTHERS)):
        peer_copies[i].wait_recv()
        total = total + peer_buf[i]
    return total, twin_copies + peer_copies


def mode_gather(group, out_ref, sems):
    twin_send, twin_recv, peer_send, peer_recv = sems
    mine = out_ref.at[:, group.me]
    peer_copies = []
    for i, (dy, dx) in enumerate(NEAR[:OTHERS]):
        target = 2 * group.chip(dy, dx) + group.core
        peer_copies.append(send(mine, mine, peer_send.at[i], peer_recv.at[i], "mode", target))
    twin_copies = [
        send(mine, mine, twin_send.at[OTHERS], twin_recv.at[OTHERS], "mode", group.twin)
    ]
    for i in reversed(range(OTHERS)):
        dy, dx = NEAR[i]
        block = out_ref.at[:, 2 * group.chip_before(dy, dx) + group.core]
        peer_copies[i].wait_recv()
        twin_copies.append(send(block, block, twin_send.at[i], twin_recv.at[i], "mode", group.twin))
    for copy in twin_copies:
        copy.wait_recv()
    return twin_copies + peer_copies


class RegionGroup:
    def __init__(self):
        self.me = lax.axis_index("region")
        self.x = self.me // Z
        self.z = self.me % Z
        self.right = self.x * Z + (self.z + 1) % Z
        self.left = self.x * Z + (self.z + Z - 1) % Z
        self.partner = (1 - self.x) * Z + self.z

    def block(self, half, z):
        side = self.x if half == 1 else 1 - self.x
        return side * Z + z % Z

    def peers(self):
        return [self.right, self.left, self.partner]


RIGHT_STEPS = Z // 2
LEFT_STEPS = Z - 1 - RIGHT_STEPS


def region_scatter(group, x_ref, right_buf, left_buf, side_buf, sems):
    right_send, right_recv, left_send, left_recv, side_send, side_recv = sems
    rights = {}
    lefts = {}

    def go_right(half, step, src):
        rights[half, step] = send(
            src, right_buf.at[half, step], right_send.at[half, step], right_recv.at[half, step],
            "region", group.right,
        )

    def go_left(half, step, src):
        lefts[half, step] = send(
            src, left_buf.at[half, step], left_send.at[half, step], left_recv.at[half, step],
            "region", group.left,
        )

    for half in (0, 1):
        go_right(half, 0, x_ref.at[:, group.block(half, group.z + RIGHT_STEPS)])
        go_left(half, 0, x_ref.at[:, group.block(half, group.z + Z - LEFT_STEPS)])
    for step in range(1, RIGHT_STEPS):
        for half in (0, 1):
            rights[half, step - 1].wait_recv()
            own = x_ref[:, group.block(half, group.z + RIGHT_STEPS - step)]
            right_buf[half, step - 1] = right_buf[half, step - 1] + own
            go_right(half, step, right_buf.at[half, step - 1])
            if step < LEFT_STEPS:
                lefts[half, step - 1].wait_recv()
                own = x_ref[:, group.block(half, group.z + Z - LEFT_STEPS + step)]
                left_buf[half, step - 1] = left_buf[half, step - 1] + own
                go_left(half, step, left_buf.at[half, step - 1])
    totals = []
    side = None
    for half in (0, 1):
        lefts[half, LEFT_STEPS - 1].wait_recv()
        own = x_ref[:, group.block(half, group.z)] + left_buf[half, LEFT_STEPS - 1]
        rights[half, RIGHT_STEPS - 1].wait_recv()
        total = own + right_buf[half, RIGHT_STEPS - 1]
        if half == 0:
            right_buf[half, RIGHT_STEPS - 1] = total
            side = send(
                right_buf.at[half, RIGHT_STEPS - 1], side_buf, side_send.at[0], side_recv.at[0],
                "region", group.partner,
            )
        else:
            totals.append(total)
    side.wait_recv()
    return totals[0] + side_buf[...], list(rights.values()) + list(lefts.values()) + [side]


def region_gather(group, src_ref, out_ref, sems):
    right_send, right_recv, left_send, left_recv, side_send, side_recv = sems
    rights = {}
    lefts = {}
    mine = out_ref.at[:, group.me]
    side = send(src_ref, mine, side_send.at[0], side_recv.at[0], "region", group.partner)
    for step in range(RIGHT_STEPS):
        for half in (1, 0):
            if step == 0 and half == 0:
                side.wait_recv()
            if step > 0:
                rights[half, step - 1].wait_recv()
            block = out_ref.at[:, group.block(half, group.z + Z - step)]
            source = src_ref if (step == 0 and half == 1) else block
            rights[half, step] = send(
                source, block, right_send.at[half, step], right_recv.at[half, step],
                "region", group.right,
            )
            if step < LEFT_STEPS:
                if step > 0:
                    lefts[half, step - 1].wait_recv()
                block = out_ref.at[:, group.block(half, group.z + step)]
                source = src_ref if (step == 0 and half == 1) else block
                lefts[half, step] = send(
                    source, block, left_send.at[half, step], left_recv.at[half, step],
                    "region", group.left,
                )
    for half in (1, 0):
        lefts[half, LEFT_STEPS - 1].wait_recv()
        rights[half, RIGHT_STEPS - 1].wait_recv()
    return list(rights.values()) + list(lefts.values()) + [side]


def finish(copies):
    for copy in copies:
        copy.wait_send()


MODE_SEMS = [DMA((OTHERS + 1,)), DMA((OTHERS + 1,)), DMA((OTHERS,)), DMA((OTHERS,))]
REGION_SEMS = [
    DMA((2, RIGHT_STEPS)), DMA((2, RIGHT_STEPS)), DMA((2, LEFT_STEPS)), DMA((2, LEFT_STEPS)),
    DMA((1,)), DMA((1,)),
]


def params(collective_id=None):
    if collective_id is None:
        return pltpu.CompilerParams(vmem_limit_bytes=56 * 2**20)
    return pltpu.CompilerParams(
        collective_id=collective_id, has_side_effects=True, vmem_limit_bytes=56 * 2**20
    )


def call(kernel, name, outs, n_smem, args, scratch=(), collective_id=None):
    return pl.pallas_call(
        kernel,
        name=name,
        out_shape=[jax.ShapeDtypeStruct(shape, f32) for shape in outs],
        in_specs=[SMEM] * n_smem + [VMEM] * (len(args) - n_smem),
        out_specs=[VMEM] * len(outs),
        scratch_shapes=list(scratch),
        compiler_params=params(collective_id),
    )(*args)


def gather_bands_kernel(object_ref, out_ref, *sems):
    group = RegionGroup()
    share = lax.axis_index("mode")
    greet("region", group.peers())
    copies = region_gather(group, object_ref.at[:, share], out_ref, sems)
    out_ref[:, group.me] = object_ref[:, share]
    finish(copies)


def gather_mode_kernel(x_ref, out_ref, *sems):
    group = ModeGroup()
    greet("mode", group.peers())
    out_ref[:, group.me] = x_ref[...]
    finish(mode_gather(group, out_ref, sems))


def reduce_mode_kernel(x_ref, out_ref, twin_buf, peer_buf, *sems):
    group = ModeGroup()
    greet("mode", group.peers())
    total, copies = mode_scatter(group, x_ref, twin_buf, peer_buf, sems[:4])
    out_ref[:, group.me] = total
    copies = copies + mode_gather(group, out_ref, sems[4:])
    finish(copies)


def scatter_mode_kernel(x_ref, out_ref, twin_buf, peer_buf, *sems):
    group = ModeGroup()
    greet("mode", group.peers())
    total, copies = mode_scatter(group, x_ref, twin_buf, peer_buf, sems)
    out_ref[...] = total
    finish(copies)


def refine_kernel(x_ref, probe_ref, out_ref, right_buf, left_buf, side_buf, *sems):
    group = RegionGroup()
    greet("region", group.peers())
    total, copies = region_scatter(group, x_ref, right_buf, left_buf, side_buf, sems[:6])
    scale = total[2:3] + 1.0
    out_ref[:, group.me] = probe_ref[:, group.me] + total[0:2] / scale
    copies = copies + region_gather(group, out_ref.at[:, group.me], out_ref, sems[6:])
    finish(copies)


def scatter_region_kernel(x_ref, out_ref, right_buf, left_buf, side_buf, *sems):
    group = RegionGroup()
    greet("region", group.peers())
    total, copies = region_scatter(group, x_ref, right_buf, left_buf, side_buf, sems)
    out_ref[...] = total
    finish(copies)


def mode_buffers(a, rows, width):
    return [pltpu.VMEM((OTHERS + 1, a, rows, width), f32), pltpu.VMEM((OTHERS, a, rows, width), f32)]


def region_buffers(a, rows, width):
    return [
        pltpu.VMEM((2, RIGHT_STEPS, a, rows, width), f32),
        pltpu.VMEM((2, LEFT_STEPS, a, rows, width), f32),
        pltpu.VMEM((a, rows, width), f32),
    ]


def frame_place(scan_ref, owner_ref, frame):
    number = lax.axis_index("region") * F_DEV + frame
    first = scan_ref[number, 0]
    anchor = first // BAND
    homes = [owner_ref[anchor + k] for k in range(3)]
    return homes, first - anchor * BAND, anchor % 2, scan_ref[number, 1]


def row_numbers(width):
    rows = lax.broadcasted_iota(jnp.int32, (SHARE, width), 0)
    return rows + lax.axis_index("mode") * SHARE


def select_kernel(scan_ref, owner_ref, bands_ref, out_ref):
    numbers = row_numbers(WIDTH)
    for frame in range(F_DEV):
        homes, lead, odd, column = frame_place(scan_ref, owner_ref, frame)
        back = (WIDTH - column) % WIDTH
        for plane in range(2):
            outer = jnp.where(numbers >= lead, bands_ref[plane, homes[0]], bands_ref[plane, homes[2]])
            inner = bands_ref[plane, homes[1]]
            outer = pltpu.roll(outer, back, 1)[:, :N]
            inner = pltpu.roll(inner, back, 1)[:, :N]
            out_ref[(frame * 2 + plane) * 2 + odd] = outer
            out_ref[(frame * 2 + plane) * 2 + 1 - odd] = inner


def place_kernel(scan_ref, owner_ref, terms_ref, out_ref):
    out_ref[...] = jnp.zeros(out_ref.shape, f32)
    numbers = row_numbers(WIDTH)
    blank = jnp.zeros((SHARE, WIDTH - N), f32)
    for frame in range(F_DEV):
        homes, lead, odd, column = frame_place(scan_ref, owner_ref, frame)
        for plane in range(2):
            outer = terms_ref[(frame * 2 + plane) * 2 + odd]
            inner = terms_ref[(frame * 2 + plane) * 2 + 1 - odd]
            outer = pltpu.roll(jnp.concatenate([outer, blank], axis=1), column, 1)
            inner = pltpu.roll(jnp.concatenate([inner, blank], axis=1), column, 1)
            out_ref[plane, homes[0]] = jnp.where(numbers >= lead, outer, 0.0)
            out_ref[plane, homes[1]] = inner
            out_ref[plane, homes[2]] = jnp.where(numbers >= lead, 0.0, outer)


def update_kernel(scan_ref, owner_ref, terms_ref, object_ref, power_ref, out_ref, tall, density):
    region = lax.axis_index("region")
    share = lax.axis_index("mode")
    own_band = lax.fori_loop(
        0, REGIONS, lambda b, found: found + jnp.where(owner_ref[b] == region, b, 0), 0
    )
    tall[0:BAND, :] = jnp.zeros((BAND, N), f32)
    tall[BAND:BAND + N, :] = power_ref[...]
    tall[BAND + N:, :] = jnp.zeros((BAND + SHARE, N), f32)
    density[...] = jnp.zeros(density.shape, f32)
    blank = jnp.zeros((SHARE, WIDTH - N), f32)

    @pl.loop(0, FRAMES)
    def _(number):
        first = scan_ref[number, 0]
        offset = own_band - first // BAND

        @pl.when(jnp.logical_and(offset >= 0, offset <= 2))
        def _():
            start = BAND + own_band * BAND - first + share * SHARE
            base = pl.multiple_of(start // 8 * 8, 8)
            rows = tall[pl.ds(base, 2 * SHARE), :]
            rows = pltpu.roll(rows, (2 * SHARE - start % 8) % (2 * SHARE), 0)[:SHARE]
            wide = jnp.concatenate([rows, blank], axis=1)
            density[...] = density[...] + pltpu.roll(wide, scan_ref[number, 1], 1)

    scale = density[...] + 1.0
    for plane in range(2):
        out_ref[plane] = object_ref[plane, share] + terms_ref[plane] / scale


def split(x):
    high = x.astype(bf16)
    low = (x - high.astype(f32)).astype(bf16)
    return high, low


def transform(real, imag, tables, sign):
    ch, cl, sh, sl = tables
    cosine = jnp.concatenate([ch, ch, cl], axis=1)
    sine = jnp.concatenate([sh, sh, sl], axis=1)
    minus = -sine
    if sign < 0:
        left_real = jnp.concatenate([cosine, sine], axis=1)
        left_imag = jnp.concatenate([minus, cosine], axis=1)
    else:
        left_real = jnp.concatenate([cosine, minus], axis=1)
        left_imag = jnp.concatenate([sine, cosine], axis=1)
    rh, rl = split(real)
    ih, il = split(imag)
    stacked = jnp.concatenate([rh, rl, rh, ih, il, ih], axis=0)
    mid_real = jnp.dot(left_real, stacked, preferred_element_type=f32)
    mid_imag = jnp.dot(left_imag, stacked, preferred_element_type=f32)
    rh, rl = split(mid_real)
    ih, il = split(mid_imag)
    beside = jnp.concatenate([rh, rl, rh, ih, il, ih], axis=1)
    cosine = jnp.concatenate([ch, ch, cl], axis=0)
    sine = jnp.concatenate([sh, sh, sl], axis=0)
    minus = -sine
    if sign < 0:
        right_real = jnp.concatenate([cosine, sine], axis=0)
        right_imag = jnp.concatenate([minus, cosine], axis=0)
    else:
        right_real = jnp.concatenate([cosine, minus], axis=0)
        right_imag = jnp.concatenate([sine, cosine], axis=0)
    return (
        jnp.dot(beside, right_real, preferred_element_type=f32),
        jnp.dot(beside, right_imag, preferred_element_type=f32),
    )


def load_tables(tables_ref):
    return tuple(tables_ref[i] for i in range(4))


def forward_waves(windows_ref, probe_ref, tables, wave_ref, out_ref):
    for frame in range(F_DEV):
        wr, wi = windows_ref[frame, 0], windows_ref[frame, 1]
        pr, pi = probe_ref[0], probe_ref[1]
        real, imag = transform(pr * wr - pi * wi, pr * wi + pi * wr, tables, -1)
        wave_ref[frame, 0] = real
        wave_ref[frame, 1] = imag
        out_ref[frame] = real * real + imag * imag


def first_wave_kernel(scan_ref, turned_ref, probe_ref, tables_ref, windows_ref, wave_ref, out_ref):
    region = lax.axis_index("region")
    for frame in range(F_DEV):
        back = (N - scan_ref[region * F_DEV + frame, 0] % N) % N
        for plane in range(2):
            windows_ref[frame, plane] = pltpu.roll(turned_ref[frame, plane], back, 0)
    forward_waves(windows_ref, probe_ref, load_tables(tables_ref), wave_ref, out_ref)


def second_wave_kernel(windows_ref, probe_ref, tables_ref, wave_ref, out_ref):
    forward_waves(windows_ref, probe_ref, load_tables(tables_ref), wave_ref, out_ref)
    out_ref[F_DEV] = probe_ref[0] * probe_ref[0] + probe_ref[1] * probe_ref[1]


def change_of(frame, wave_ref, intensity_ref, measured_ref, tables):
    factor = jnp.sqrt(measured_ref[frame]) / jnp.sqrt(intensity_ref[frame] + 0.1) - 1.0
    return transform(wave_ref[frame, 0] * factor, wave_ref[frame, 1] * factor, tables, 1)


def gradient_kernel(wave_ref, intensity_ref, measured_ref, windows_ref, tables_ref, out_ref):
    tables = load_tables(tables_ref)
    for frame in range(F_DEV):
        cr, ci = change_of(frame, wave_ref, intensity_ref, measured_ref, tables)
        wr, wi = windows_ref[frame, 0], windows_ref[frame, 1]
        parts = (wr * cr + wi * ci, wr * ci - wi * cr, wr * wr + wi * wi)
        for k, part in enumerate(parts):
            out_ref[k] = part if frame == 0 else out_ref[k] + part


def terms_kernel(scan_ref, wave_ref, intensity_ref, measured_ref, probe_ref, tables_ref, out_ref):
    region = lax.axis_index("region")
    tables = load_tables(tables_ref)
    for frame in range(F_DEV):
        cr, ci = change_of(frame, wave_ref, intensity_ref, measured_ref, tables)
        pr, pi = probe_ref[0], probe_ref[1]
        turn = scan_ref[region * F_DEV + frame, 0] % N
        out_ref[frame, 0] = pltpu.roll(pr * cr + pi * ci, turn, 0)
        out_ref[frame, 1] = pltpu.roll(pr * ci - pi * cr, turn, 0)


def table_array():
    product = np.arange(N)[:, None] * np.arange(N)[None, :] % N
    angles = product * (2.0 * math.pi / N)
    pieces = []
    for values in (np.cos(angles) / 16.0, np.sin(angles) / 16.0):
        high = values.astype(bf16)
        pieces += [high, (values - high.astype(np.float64)).astype(bf16)]
    return np.stack(pieces)


def body(measured, probe_modes, object_bands, scan_offsets, band_owner):
    tables = jnp.asarray(table_array())
    probe = probe_modes[:, 0]
    shares = object_bands.reshape(2, MODES, SHARE, WIDTH)
    image_shape = (2, REGIONS, SHARE, WIDTH)
    (bands,) = call(gather_bands_kernel, "gather_bands", [image_shape], 0, [shares], REGION_SEMS, 1)
    (chosen,) = call(
        select_kernel, "select", [(8, SHARE, N)], 2, [scan_offsets, band_owner, bands]
    )
    (turned,) = call(gather_mode_kernel, "gather_windows", [(8, MODES, SHARE, N)], 0, [chosen], MODE_SEMS, 2)
    frame_shape = (F_DEV, 2, N, N)
    windows, wave, intensity = call(
        first_wave_kernel, "first_wave", [frame_shape, frame_shape, (F_DEV, N, N)], 1,
        [scan_offsets, turned.reshape(frame_shape), probe, tables],
    )
    (summed,) = call(
        reduce_mode_kernel, "sum_intensity", [(2, MODES, 16, N)], 0,
        [intensity.reshape(2, MODES, 16, N)], mode_buffers(2, 16, N) + MODE_SEMS * 2, 3,
    )
    (gradient,) = call(
        gradient_kernel, "gradient", [(3, N, N)], 0,
        [wave, summed.reshape(F_DEV, N, N), measured, windows, tables],
    )
    (probe,) = call(
        refine_kernel, "refine", [(2, REGIONS, 8, N)], 0,
        [gradient.reshape(3, REGIONS, 8, N), probe.reshape(2, REGIONS, 8, N)],
        region_buffers(3, 8, N) + REGION_SEMS * 2, 4,
    )
    probe = probe.reshape(2, N, N)
    wave, intensity = call(
        second_wave_kernel, "second_wave", [frame_shape, (F_DEV + 1, N, N)], 0,
        [windows, probe, tables],
    )
    (summed,) = call(
        reduce_mode_kernel, "sum_second", [(3, MODES, 16, N)], 0,
        [intensity.reshape(3, MODES, 16, N)], mode_buffers(3, 16, N) + MODE_SEMS * 2, 5,
    )
    summed = summed.reshape(3, N, N)
    (terms,) = call(
        terms_kernel, "terms", [frame_shape], 1,
        [scan_offsets, wave, summed, measured, probe, tables],
    )
    (terms,) = call(
        scatter_mode_kernel, "scatter_terms", [(8, SHARE, N)], 0,
        [terms.reshape(8, MODES, SHARE, N)], mode_buffers(8, SHARE, N) + MODE_SEMS, 6,
    )
    (placed,) = call(
        place_kernel, "place", [image_shape], 2, [scan_offsets, band_owner, terms]
    )
    (update,) = call(
        scatter_region_kernel, "scatter_update", [(2, SHARE, WIDTH)], 0, [placed],
        region_buffers(2, SHARE, WIDTH) + REGION_SEMS, 7,
    )
    (rows,) = call(
        update_kernel, "update", [(2, SHARE, WIDTH)], 2,
        [scan_offsets, band_owner, update, shares, summed[F_DEV]],
        [pltpu.VMEM((2 * BAND + N + SHARE, N), f32), pltpu.VMEM((SHARE, WIDTH), f32)],
    )
    (object_out,) = call(
        gather_mode_kernel, "gather_rows", [(2, MODES, SHARE, WIDTH)], 0, [rows], MODE_SEMS, 8
    )
    return probe[:, None], object_out.reshape(2, BAND, WIDTH)


def solution(mesh):
    in_specs = (
        P("region", None, None),
        P(None, "mode", None, None),
        P(None, "region", None),
        P(),
        P(),
    )
    out_specs = (P(None, "mode", None, None), P(None, "region", None))
    return jax.shard_map(body, mesh=mesh, in_specs=in_specs, out_specs=out_specs, check_vma=False)
```

```python
import functools
import math

import jax
import jax.numpy as jnp
import numpy as np
from jax import lax
from jax.experimental import pallas as pl
from jax.experimental.pallas import tpu as pltpu
from jax.sharding import PartitionSpec as P

N = 256
BAND = 128
WIDTH = 512
FRAMES = 64
F_DEV = 2
REGIONS = 32
MODES = 16
Z = 16
Y = 4
SHARE = BAND // MODES
TURNS = 8
f32 = jnp.float32
bf16 = jnp.bfloat16

VMEM = pl.BlockSpec(memory_space=pltpu.VMEM)
SMEM = pl.BlockSpec(memory_space=pltpu.SMEM)
DMA = pltpu.SemaphoreType.DMA

NEAR = ((2, 1), (2, 0), (1, 1), (3, 1), (1, 0), (3, 0), (0, 1), (0, 0))
OTHERS = len(NEAR) - 1


def send(src, dst, send_sem, recv_sem, axis, index):
    copy = pltpu.make_async_remote_copy(
        src_ref=src,
        dst_ref=dst,
        send_sem=send_sem,
        recv_sem=recv_sem,
        device_id={axis: index},
        device_id_type=pl.DeviceIdType.MESH,
    )
    copy.start()
    return copy


def greet(peers):
    barrier = pltpu.get_barrier_semaphore()
    for axis, peer in peers:
        pl.semaphore_signal(
            barrier, inc=1, device_id={axis: peer}, device_id_type=pl.DeviceIdType.MESH
        )
    pl.semaphore_wait(barrier, len(peers))


class ModeGroup:
    def __init__(self):
        self.me = lax.axis_index("mode")
        self.y = self.me // 4
        self.x = (self.me // 2) % 2
        self.core = self.me % 2
        self.twin = self.me + 1 - 2 * self.core

    def chip(self, dy, dx):
        return ((self.y + dy) % Y) * 2 + (self.x + dx) % 2

    def chip_before(self, dy, dx):
        return ((self.y + Y - dy) % Y) * 2 + (self.x + 2 - dx) % 2

    def peers(self):
        chips = [2 * self.chip(dy, dx) + self.core for dy, dx in NEAR[:OTHERS]]
        return [("mode", peer) for peer in chips + [self.twin]]


def mode_scatter(group, x_ref, twin_buf, peer_buf, sems, copies):
    twin_send, twin_recv, peer_send, peer_recv = sems
    twin_copies = []
    for i, (dy, dx) in enumerate(NEAR):
        block = 2 * group.chip(dy, dx) + 1 - group.core
        twin_copies.append(
            send(x_ref.at[:, block], twin_buf.at[i], twin_send.at[i], twin_recv.at[i], "mode", group.twin)
        )
    yield
    peer_copies = []
    for i, (dy, dx) in enumerate(NEAR):
        target = 2 * group.chip(dy, dx) + group.core
        twin_copies[i].wait_recv()
        twin_buf[i] = twin_buf[i] + x_ref[:, target]
        if i < OTHERS:
            peer_copies.append(
                send(twin_buf.at[i], peer_buf.at[i], peer_send.at[i], peer_recv.at[i], "mode", target)
            )
    yield
    total = twin_buf[OTHERS]
    for i in reversed(range(OTHERS)):
        peer_copies[i].wait_recv()
        total = total + peer_buf[i]
    copies += twin_copies + peer_copies
    return total


def mode_gather(group, out_ref, sems, copies):
    twin_send, twin_recv, peer_send, peer_recv = sems
    mine = out_ref.at[:, group.me]
    peer_copies = []
    for i, (dy, dx) in enumerate(NEAR[:OTHERS]):
        target = 2 * group.chip(dy, dx) + group.core
        peer_copies.append(send(mine, mine, peer_send.at[i], peer_recv.at[i], "mode", target))
    twin_copies = [
        send(mine, mine, twin_send.at[OTHERS], twin_recv.at[OTHERS], "mode", group.twin)
    ]
    yield
    for i in reversed(range(OTHERS)):
        dy, dx = NEAR[i]
        block = out_ref.at[:, 2 * group.chip_before(dy, dx) + group.core]
        peer_copies[i].wait_recv()
        twin_copies.append(send(block, block, twin_send.at[i], twin_recv.at[i], "mode", group.twin))
    yield
    for copy in twin_copies:
        copy.wait_recv()
    copies += twin_copies + peer_copies


class RegionGroup:
    def __init__(self):
        self.me = lax.axis_index("region")
        self.x = self.me // Z
        self.z = self.me % Z
        self.partner = (1 - self.x) * Z + self.z

    def at(self, step):
        return self.x * Z + (self.z + step % Z) % Z

    def block(self, half, step):
        side = self.x if half == 1 else 1 - self.x
        return side * Z + (self.z + step % Z) % Z

    def peers(self):
        return [("region", self.block(half, step)) for half, step in ALL]


FAR = (8, 4, 12)
NEXT = (1, -1, 2, -2)


ALL = tuple(
    (half, step)
    for step in (8, 7, 9, 6, 10, 5, 11, 4, 12, 3, 13, 2, 14, 1, 15, 0)
    for half in ((0, 1) if step else (0,))
)


def neighbours(step):
    return NEXT if step % 8 == 0 else NEXT[:2]


def region_scatter(group, x_ref, near_buf, far_buf, side_buf, sems, copies):
    near_send, near_recv, far_send, far_recv, side_send, side_recv = sems
    near = {}
    far = {}
    for half in (0, 1):
        for e, step in enumerate((*FAR, 0)):
            for t, turn in enumerate(neighbours(step)):
                near[half, e, t] = send(
                    x_ref.at[:, group.block(half, turn + step)], near_buf.at[half, e, t],
                    near_send.at[half, e, t], near_recv.at[half, e, t], "region", group.at(turn),
                )
    yield
    for half in (0, 1):
        for e, step in enumerate((*FAR, 0)):
            total = x_ref[:, group.block(half, step)]
            for t in range(len(neighbours(step))):
                near[half, e, t].wait_recv()
                total = total + near_buf[half, e, t]
            near_buf[half, e, 0] = total
            if step:
                far[half, e] = send(
                    near_buf.at[half, e, 0], far_buf.at[half, e], far_send.at[half, e],
                    far_recv.at[half, e], "region", group.at(step),
                )
    yield
    side = None
    for half in (0, 1):
        total = near_buf[half, len(FAR), 0]
        for e in reversed(range(len(FAR))):
            far[half, e].wait_recv()
            total = total + far_buf[half, e]
        near_buf[half, len(FAR), 0] = total
        if half == 0:
            side = send(
                near_buf.at[half, len(FAR), 0], side_buf, side_send.at[0], side_recv.at[0],
                "region", group.partner,
            )
    yield
    side.wait_recv()
    copies += list(near.values()) + list(far.values()) + [side]
    return near_buf[1, len(FAR), 0] + side_buf[...]


def region_gather(group, out_ref, sems, copies):
    near_send, near_recv, far_send, far_recv, side_send, side_recv = sems
    near = {}
    far = {}
    mine = out_ref.at[:, group.me]
    side = send(mine, mine, side_send.at[0], side_recv.at[0], "region", group.partner)

    def go_near(half, e, step):
        block = out_ref.at[:, group.block(half, -step)]
        for t, turn in enumerate(neighbours(step)):
            near[half, e, t] = send(
                block, block, near_send.at[half, e, t], near_recv.at[half, e, t],
                "region", group.at(turn),
            )

    for half in (1, 0):
        block = out_ref.at[:, group.block(half, 0)]
        if half == 0:
            side.wait_recv()
        for e, step in enumerate(FAR):
            far[half, e] = send(
                block, block, far_send.at[half, e], far_recv.at[half, e], "region", group.at(step)
            )
        go_near(half, len(FAR), 0)
    yield
    for half in (1, 0):
        for e in reversed(range(len(FAR))):
            far[half, e].wait_recv()
            go_near(half, e, FAR[e])
    yield
    for copy in near.values():
        copy.wait_recv()
    copies += list(near.values()) + list(far.values()) + [side]


def region_exchange(group, x_ref, out_ref, sems, copies):
    send_sem, recv_sem = sems
    begun = []
    for i, (half, step) in enumerate(ALL):
        target = group.block(half, step)
        begun.append(
            send(
                x_ref.at[:, target], out_ref.at[:, group.me], send_sem.at[i], recv_sem.at[i],
                "region", target,
            )
        )
    out_ref[:, group.me] = x_ref[:, group.me]
    yield
    for copy in begun:
        copy.wait_recv()
    copies += begun


def run(steps):
    while True:
        try:
            next(steps)
        except StopIteration as end:
            return end.value


def advance(steps):
    next(steps)


def mode_buffers(a, rows, width):
    return [pltpu.VMEM((OTHERS + 1, a, rows, width), f32), pltpu.VMEM((OTHERS, a, rows, width), f32)]


def region_buffers(a, rows, width):
    return [
        pltpu.VMEM((2, 4, 4, a, rows, width), f32),
        pltpu.VMEM((2, 3, a, rows, width), f32),
        pltpu.VMEM((a, rows, width), f32),
    ]


MODE_SEMS = [DMA((OTHERS + 1,)), DMA((OTHERS + 1,)), DMA((OTHERS,)), DMA((OTHERS,))]
REGION_SEMS = [DMA((2, 4, 4)), DMA((2, 4, 4)), DMA((2, 3)), DMA((2, 3)), DMA((1,)), DMA((1,))]
EXCHANGE_SEMS = [DMA((len(ALL),)), DMA((len(ALL),))]


def own_band_of(owner_ref):
    region = lax.axis_index("region")
    found = 0
    for band in range(REGIONS):
        found = found + jnp.where(owner_ref[band] == region, band, 0)
    return found


def touching_frame(scan_ref, own_band, region):
    firsts = [scan_ref[region * F_DEV + frame, 0] for frame in range(F_DEV)]
    columns = [scan_ref[region * F_DEV + frame, 1] for frame in range(F_DEV)]
    gaps = [own_band - first // BAND for first in firsts]
    covers = [jnp.logical_and(gap >= 0, gap <= 2) for gap in gaps]
    first = jnp.where(covers[0], firsts[0], firsts[1])
    column = jnp.where(covers[0], columns[0], columns[1])
    return first, column, jnp.logical_or(covers[0], covers[1])


def prepare(scan_ref, owner_ref, object_ref, packed, table, bits):
    share = lax.axis_index("mode")
    own_band = own_band_of(owner_ref)

    @pl.loop(0, REGIONS)
    def _(region):
        _, column, _ = touching_frame(scan_ref, own_band, region)
        for plane in range(2):
            rows = pltpu.roll(object_ref[plane, share], (WIDTH - column) % WIDTH, 1)
            packed[plane, region] = rows[:, :N]

    numbers = lax.broadcasted_iota(jnp.int32, (SHARE, N), 0) + share * SHARE
    for frame in range(F_DEV):
        first = scan_ref[lax.axis_index("region") * F_DEV + frame, 0]
        anchor = first // BAND
        homes = [owner_ref[anchor + k] for k in range(3)]
        outer = jnp.where(numbers >= first - anchor * BAND, homes[0], homes[2])
        inner = jnp.full((SHARE, N), homes[1], jnp.int32)
        odd = jnp.full((SHARE, N), anchor % 2, jnp.int32) == 1
        table[frame * 2] = jnp.where(odd, inner, outer)
        table[frame * 2 + 1] = jnp.where(odd, outer, inner)
        for k in range(TURNS):
            bits[frame * TURNS + k] = jnp.full((1, N), first // 2**k % 2, jnp.int32)


def select_rows(table, bands, out_ref):
    share = lax.axis_index("mode")
    for frame in range(F_DEV):
        for half in range(2):
            homes = table[frame * 2 + half]
            rows = [bands[plane, 0] for plane in range(2)]
            for block in range(1, REGIONS):
                here = homes == block
                rows = [jnp.where(here, bands[plane, block], rows[plane]) for plane in range(2)]
            for plane in range(2):
                out_ref[(frame * 2 + plane) * 2 + half, share] = rows[plane]


def place_terms(table, terms, out_ref):
    for block in range(REGIONS):
        rows = [jnp.zeros((SHARE, N), f32) for plane in range(2)]
        for frame in range(F_DEV):
            for half in range(2):
                here = table[frame * 2 + half] == block
                rows = [
                    jnp.where(here, terms[(frame * 2 + plane) * 2 + half], rows[plane])
                    for plane in range(2)
                ]
        for plane in range(2):
            out_ref[plane, block] = rows[plane]


def turn_rows(values, bits, frame, back):
    for k in range(TURNS):
        here = jnp.broadcast_to(bits[frame * TURNS + k], (N, N)) == 1
        shift = N - 2**k if back else 2**k
        if shift % 8 == 0:
            rolled = [jnp.concatenate([v[N - shift:], v[:N - shift]], axis=0) for v in values]
        else:
            rolled = [pltpu.roll(v, shift, 0) for v in values]
        values = [jnp.where(here, r, v) for r, v in zip(rolled, values)]
    return values


def update_kernel(scan_ref, owner_ref, parts_ref, object_ref, power_ref, out_ref, tall, placed):
    share = lax.axis_index("mode")
    own_band = own_band_of(owner_ref)
    tall[0:BAND, :] = jnp.zeros((BAND, N), f32)
    tall[BAND:BAND + N, :] = power_ref[...]
    tall[BAND + N:, :] = jnp.zeros((BAND + SHARE, N), f32)
    placed[...] = jnp.zeros(placed.shape, f32)
    blank = jnp.zeros((SHARE, WIDTH - N), f32)

    @pl.loop(0, REGIONS)
    def _(region):
        first, column, covers = touching_frame(scan_ref, own_band, region)
        start = jnp.where(covers, BAND + own_band * BAND - first, 0) + share * SHARE
        base = pl.multiple_of(start // 8 * 8, 8)
        rows = pltpu.roll(tall[pl.ds(base, 2 * SHARE), :], (2 * SHARE - start % 8) % (2 * SHARE), 0)
        rows = jnp.where(covers, rows[:SHARE], 0.0)
        for k, part in enumerate((parts_ref[0, region], parts_ref[1, region], rows)):
            wide = pltpu.roll(jnp.concatenate([part, blank], axis=1), column, 1)
            placed[k] = placed[k] + wide

    scale = placed[2] + 1.0
    for plane in range(2):
        out_ref[plane] = object_ref[plane, share] + placed[plane] / scale


def gather_rows_kernel(x_ref, out_ref, *sems):
    group = ModeGroup()
    copies = []
    greet(group.peers())
    out_ref[:, group.me] = x_ref[...]
    run(mode_gather(group, out_ref, sems, copies))
    for copy in copies:
        copy.wait_send()


def split(x):
    high = x.astype(bf16)
    low = (x - high.astype(f32)).astype(bf16)
    return high, low


def transform(real, imag, tables, sign):
    ch, cl, sh, sl = tables
    cosine = jnp.concatenate([ch, ch, cl], axis=1)
    sine = jnp.concatenate([sh, sh, sl], axis=1)
    minus = -sine
    if sign < 0:
        left_real = jnp.concatenate([cosine, sine], axis=1)
        left_imag = jnp.concatenate([minus, cosine], axis=1)
    else:
        left_real = jnp.concatenate([cosine, minus], axis=1)
        left_imag = jnp.concatenate([sine, cosine], axis=1)
    rh, rl = split(real)
    ih, il = split(imag)
    stacked = jnp.concatenate([rh, rl, rh, ih, il, ih], axis=0)
    mid_real = jnp.dot(left_real, stacked, preferred_element_type=f32)
    mid_imag = jnp.dot(left_imag, stacked, preferred_element_type=f32)
    rh, rl = split(mid_real)
    ih, il = split(mid_imag)
    beside = jnp.concatenate([rh, rl, rh, ih, il, ih], axis=1)
    cosine = jnp.concatenate([ch, ch, cl], axis=0)
    sine = jnp.concatenate([sh, sh, sl], axis=0)
    minus = -sine
    if sign < 0:
        right_real = jnp.concatenate([cosine, sine], axis=0)
        right_imag = jnp.concatenate([minus, cosine], axis=0)
    else:
        right_real = jnp.concatenate([cosine, minus], axis=0)
        right_imag = jnp.concatenate([sine, cosine], axis=0)
    return (
        jnp.dot(beside, right_real, preferred_element_type=f32),
        jnp.dot(beside, right_imag, preferred_element_type=f32),
    )


def load_tables(tables_ref):
    return tuple(tables_ref[i] for i in range(4))


def blocks(value, count):
    return value.reshape(count, N // count, N)


def whole(ref, k):
    return ref[k].reshape(N, N)


def program(
    packed, table, bits, probe_ref, measured_ref, tables_ref, probe_out, arrived, mode_power,
    bands, turned, windows, waves, power, intensity, summed, gradient, terms, parts, *rest,
):
    rest = list(rest)

    def take(count):
        taken = rest[:count]
        del rest[:count]
        return taken

    mode = ModeGroup()
    region = RegionGroup()
    copies = []
    tables = load_tables(tables_ref)

    greet(mode.peers() + region.peers())
    run(region_exchange(region, packed, bands, take(2), copies))
    select_rows(table, bands, turned)
    run(mode_gather(mode, turned, take(4), copies))
    total = jnp.zeros((N, N), f32)
    for frame in range(F_DEV):
        values = [turned[k:k + 2].reshape(N, N) for k in (frame * 4, frame * 4 + 2)]
        for plane, value in enumerate(turn_rows(values, bits, frame, True)):
            windows[frame, plane] = value
            total = total + value * value
    power[0] = blocks(total, REGIONS)
    power_steps = region_scatter(region, power, *take(3), take(6), copies)
    advance(power_steps)

    def forward(frame, pr, pi):
        wr, wi = windows[frame, 0], windows[frame, 1]
        real, imag = transform(pr * wr - pi * wi, pr * wi + pi * wr, tables, -1)
        waves[frame, 0] = real
        waves[frame, 1] = imag
        intensity[frame] = blocks(real * real + imag * imag, MODES)

    def change(frame):
        factor = jnp.sqrt(measured_ref[frame]) / jnp.sqrt(whole(summed, frame) + 0.1) - 1.0
        return transform(waves[frame, 0] * factor, waves[frame, 1] * factor, tables, 1)

    pr, pi = whole(probe_ref, 0), whole(probe_ref, 1)
    forward(0, pr, pi)
    forward(1, pr, pi)
    first_two = (pl.ds(0, F_DEV),)
    sums = mode_scatter(mode, intensity.at[first_two], *take(2), take(4), copies)
    advance(sums)
    advance(power_steps)
    total = run(sums)
    for frame in range(F_DEV):
        summed[frame, mode.me] = total[frame]
    gathers = mode_gather(mode, summed.at[first_two], take(4), copies)
    advance(gathers)
    advance(power_steps)
    run(gathers)
    power_total = run(power_steps)
    grad_real = jnp.zeros((N, N), f32)
    grad_imag = jnp.zeros((N, N), f32)
    for frame in range(F_DEV):
        cr, ci = change(frame)
        wr, wi = windows[frame, 0], windows[frame, 1]
        grad_real = grad_real + (wr * cr + wi * ci)
        grad_imag = grad_imag + (wr * ci - wi * cr)
    gradient[0] = blocks(grad_real, REGIONS)
    gradient[1] = blocks(grad_imag, REGIONS)
    total = run(region_scatter(region, gradient, *take(3), take(6), copies))
    probe_out[:, region.me] = probe_ref[:, region.me] + total / (power_total + 1.0)
    run(region_gather(region, probe_out, take(6), copies))

    pr, pi = whole(probe_out, 0), whole(probe_out, 1)
    intensity_again, summed_again = take(2)
    intensity = intensity_again
    summed = summed_again
    forward(0, pr, pi)
    forward(1, pr, pi)
    intensity[F_DEV] = blocks(pr * pr + pi * pi, MODES)
    total = run(mode_scatter(mode, intensity, *take(2), take(4), copies))
    summed[:, mode.me] = total
    run(mode_gather(mode, summed, take(4), copies))
    for frame in range(F_DEV):
        cr, ci = change(frame)
        values = [pr * cr + pi * ci, pr * ci - pi * cr]
        for plane, value in enumerate(turn_rows(values, bits, frame, False)):
            k = frame * 4 + plane * 2
            terms[k:k + 2] = value.reshape(2, MODES, SHARE, N)
    total = run(mode_scatter(mode, terms, *take(2), take(4), copies))
    place_terms(table, total, parts)
    run(region_exchange(region, parts, arrived, take(2), copies))
    mode_power[...] = whole(summed, F_DEV)
    for copy in copies:
        copy.wait_send()


def vmem(*shape):
    return pltpu.VMEM(shape, f32)


SCRATCH = [
    vmem(2, REGIONS, SHARE, N),
    vmem(8, MODES, SHARE, N),
    vmem(F_DEV, 2, N, N),
    vmem(F_DEV, 2, N, N),
    vmem(1, REGIONS, 8, N),
    vmem(F_DEV, MODES, 16, N),
    vmem(F_DEV, MODES, 16, N),
    vmem(2, REGIONS, 8, N),
    vmem(8, MODES, SHARE, N),
    vmem(2, REGIONS, SHARE, N),
    *EXCHANGE_SEMS,
    *MODE_SEMS,
    *region_buffers(1, 8, N), *REGION_SEMS,
    *mode_buffers(F_DEV, 16, N), *MODE_SEMS,
    *MODE_SEMS,
    *region_buffers(2, 8, N), *REGION_SEMS,
    *REGION_SEMS,
    vmem(F_DEV + 1, MODES, 16, N), vmem(F_DEV + 1, MODES, 16, N),
    *mode_buffers(F_DEV + 1, 16, N), *MODE_SEMS,
    *MODE_SEMS,
    *mode_buffers(8, SHARE, N), *MODE_SEMS,
    *EXCHANGE_SEMS,
]


def call(kernel, name, outs, n_smem, args, scratch=(), collective_id=None):
    params = pltpu.CompilerParams(vmem_limit_bytes=60 * 2**20)
    if collective_id is not None:
        params = pltpu.CompilerParams(
            collective_id=collective_id, has_side_effects=True, vmem_limit_bytes=60 * 2**20
        )
    return pl.pallas_call(
        kernel,
        name=name,
        out_shape=[jax.ShapeDtypeStruct(*out) for out in outs],
        in_specs=[SMEM] * n_smem + [VMEM] * (len(args) - n_smem),
        out_specs=[VMEM] * len(outs),
        scratch_shapes=list(scratch),
        compiler_params=params,
    )(*args)


def body(measured, probe_modes, object_bands, scan_offsets, band_owner):
    shares = object_bands.reshape(2, MODES, SHARE, WIDTH)
    exchanged = ((2, REGIONS, SHARE, N), f32)
    packed, table, bits = call(
        prepare, "prepare",
        [exchanged, ((2 * F_DEV, SHARE, N), jnp.int32), ((F_DEV * TURNS, 1, N), jnp.int32)],
        2, [scan_offsets, band_owner, shares],
    )
    probe, arrived, power = call(
        program, "ptychography", [((2, REGIONS, 8, N), f32), exchanged, ((N, N), f32)], 0,
        [packed, table, bits, probe_modes.reshape(2, REGIONS, 8, N), measured, jnp.asarray(table_array())],
        SCRATCH, 1,
    )
    (rows,) = call(
        update_kernel, "update", [((2, SHARE, WIDTH), f32)], 2,
        [scan_offsets, band_owner, arrived, shares, power],
        [vmem(2 * BAND + N + SHARE, N), vmem(3, SHARE, WIDTH)],
    )
    (object_out,) = call(
        gather_rows_kernel, "gather_rows", [((2, MODES, SHARE, WIDTH), f32)], 0, [rows], MODE_SEMS, 2
    )
    return probe.reshape(2, 1, N, N), object_out.reshape(2, BAND, WIDTH)


def table_array():
    product = np.arange(N)[:, None] * np.arange(N)[None, :] % N
    angles = product * (2.0 * math.pi / N)
    pieces = []
    for values in (np.cos(angles) / 16.0, np.sin(angles) / 16.0):
        high = values.astype(bf16)
        pieces += [high, (values - high.astype(np.float64)).astype(bf16)]
    return np.stack(pieces)


def solution(mesh):
    in_specs = (
        P("region", None, None),
        P(None, "mode", None, None),
        P(None, "region", None),
        P(),
        P(),
    )
    out_specs = (P(None, "mode", None, None), P(None, "region", None))
    return jax.shard_map(body, mesh=mesh, in_specs=in_specs, out_specs=out_specs, check_vma=False)
```

```python
import functools
import math

import jax
import jax.numpy as jnp
import numpy as np
from jax import lax
from jax.experimental import pallas as pl
from jax.experimental.pallas import tpu as pltpu
from jax.sharding import PartitionSpec as P

N = 256
BAND = 128
WIDTH = 512
FRAMES = 64
F_DEV = 2
REGIONS = 32
MODES = 16
Z = 16
Y = 4
SHARE = BAND // MODES
TURNS = 8
f32 = jnp.float32
bf16 = jnp.bfloat16

VMEM = pl.BlockSpec(memory_space=pltpu.VMEM)
SMEM = pl.BlockSpec(memory_space=pltpu.SMEM)
DMA = pltpu.SemaphoreType.DMA

NEAR = ((2, 1), (2, 0), (1, 1), (3, 1), (1, 0), (3, 0), (0, 1), (0, 0))
OTHERS = len(NEAR) - 1


def send(src, dst, send_sem, recv_sem, axis, index):
    copy = pltpu.make_async_remote_copy(
        src_ref=src,
        dst_ref=dst,
        send_sem=send_sem,
        recv_sem=recv_sem,
        device_id={axis: index},
        device_id_type=pl.DeviceIdType.MESH,
    )
    copy.start()
    return copy


def greet(peers):
    barrier = pltpu.get_barrier_semaphore()
    for axis, peer in peers:
        pl.semaphore_signal(
            barrier, inc=1, device_id={axis: peer}, device_id_type=pl.DeviceIdType.MESH
        )
    pl.semaphore_wait(barrier, len(peers))


class ModeGroup:
    def __init__(self):
        self.me = lax.axis_index("mode")
        self.y = self.me // 4
        self.x = (self.me // 2) % 2
        self.core = self.me % 2
        self.twin = self.me + 1 - 2 * self.core

    def chip(self, dy, dx):
        return ((self.y + dy) % Y) * 2 + (self.x + dx) % 2

    def chip_before(self, dy, dx):
        return ((self.y + Y - dy) % Y) * 2 + (self.x + 2 - dx) % 2

    def peers(self):
        chips = [2 * self.chip(dy, dx) + self.core for dy, dx in NEAR[:OTHERS]]
        return [("mode", peer) for peer in chips + [self.twin]]


def mode_scatter(group, x_ref, twin_buf, peer_buf, sems, copies):
    twin_send, twin_recv, peer_send, peer_recv = sems
    twin_copies = []
    for i, (dy, dx) in enumerate(NEAR):
        block = 2 * group.chip(dy, dx) + 1 - group.core
        twin_copies.append(
            send(x_ref.at[:, block], twin_buf.at[i], twin_send.at[i], twin_recv.at[i], "mode", group.twin)
        )
    yield
    peer_copies = []
    for i, (dy, dx) in enumerate(NEAR):
        target = 2 * group.chip(dy, dx) + group.core
        twin_copies[i].wait_recv()
        twin_buf[i] = twin_buf[i] + x_ref[:, target]
        if i < OTHERS:
            peer_copies.append(
                send(twin_buf.at[i], peer_buf.at[i], peer_send.at[i], peer_recv.at[i], "mode", target)
            )
    yield
    total = twin_buf[OTHERS]
    for i in reversed(range(OTHERS)):
        peer_copies[i].wait_recv()
        total = total + peer_buf[i]
    copies += twin_copies + peer_copies
    return total


def mode_gather(group, out_ref, sems, copies):
    twin_send, twin_recv, peer_send, peer_recv = sems
    mine = out_ref.at[:, group.me]
    peer_copies = []
    for i, (dy, dx) in enumerate(NEAR[:OTHERS]):
        target = 2 * group.chip(dy, dx) + group.core
        peer_copies.append(send(mine, mine, peer_send.at[i], peer_recv.at[i], "mode", target))
    twin_copies = [
        send(mine, mine, twin_send.at[OTHERS], twin_recv.at[OTHERS], "mode", group.twin)
    ]
    yield
    for i in reversed(range(OTHERS)):
        dy, dx = NEAR[i]
        block = out_ref.at[:, 2 * group.chip_before(dy, dx) + group.core]
        peer_copies[i].wait_recv()
        twin_copies.append(send(block, block, twin_send.at[i], twin_recv.at[i], "mode", group.twin))
    yield
    for copy in twin_copies:
        copy.wait_recv()
    copies += twin_copies + peer_copies


class RegionGroup:
    def __init__(self):
        self.me = lax.axis_index("region")
        self.x = self.me // Z
        self.z = self.me % Z
        self.partner = (1 - self.x) * Z + self.z

    def at(self, step):
        return self.x * Z + (self.z + step % Z) % Z

    def block(self, half, step):
        side = self.x if half == 1 else 1 - self.x
        return side * Z + (self.z + step % Z) % Z

    def peers(self):
        return [("region", self.block(half, step)) for half, step in ALL]


FAR = (8, 4, 12)
NEXT = (1, -1, 2, -2)


ALL = tuple(
    (half, step)
    for step in (8, 7, 9, 6, 10, 5, 11, 4, 12, 3, 13, 2, 14, 1, 15, 0)
    for half in ((0, 1) if step else (0,))
)


def neighbours(step):
    return NEXT if step % 8 == 0 else NEXT[:2]


def region_scatter(group, x_ref, near_buf, far_buf, side_buf, sems, copies):
    near_send, near_recv, far_send, far_recv, side_send, side_recv = sems
    near = {}
    far = {}
    for half in (0, 1):
        for e, step in enumerate((*FAR, 0)):
            for t, turn in enumerate(neighbours(step)):
                near[half, e, t] = send(
                    x_ref.at[:, group.block(half, turn + step)], near_buf.at[half, e, t],
                    near_send.at[half, e, t], near_recv.at[half, e, t], "region", group.at(turn),
                )
    yield
    for half in (0, 1):
        for e, step in enumerate((*FAR, 0)):
            total = x_ref[:, group.block(half, step)]
            for t in range(len(neighbours(step))):
                near[half, e, t].wait_recv()
                total = total + near_buf[half, e, t]
            near_buf[half, e, 0] = total
            if step:
                far[half, e] = send(
                    near_buf.at[half, e, 0], far_buf.at[half, e], far_send.at[half, e],
                    far_recv.at[half, e], "region", group.at(step),
                )
    yield
    side = None
    for half in (0, 1):
        total = near_buf[half, len(FAR), 0]
        for e in reversed(range(len(FAR))):
            far[half, e].wait_recv()
            total = total + far_buf[half, e]
        near_buf[half, len(FAR), 0] = total
        if half == 0:
            side = send(
                near_buf.at[half, len(FAR), 0], side_buf, side_send.at[0], side_recv.at[0],
                "region", group.partner,
            )
    yield
    side.wait_recv()
    copies += list(near.values()) + list(far.values()) + [side]
    return near_buf[1, len(FAR), 0] + side_buf[...]


def region_gather(group, out_ref, sems, copies):
    near_send, near_recv, far_send, far_recv, side_send, side_recv = sems
    near = {}
    far = {}
    mine = out_ref.at[:, group.me]
    side = send(mine, mine, side_send.at[0], side_recv.at[0], "region", group.partner)

    def go_near(half, e, step):
        block = out_ref.at[:, group.block(half, -step)]
        for t, turn in enumerate(neighbours(step)):
            near[half, e, t] = send(
                block, block, near_send.at[half, e, t], near_recv.at[half, e, t],
                "region", group.at(turn),
            )

    for half in (1, 0):
        block = out_ref.at[:, group.block(half, 0)]
        if half == 0:
            side.wait_recv()
        for e, step in enumerate(FAR):
            far[half, e] = send(
                block, block, far_send.at[half, e], far_recv.at[half, e], "region", group.at(step)
            )
        go_near(half, len(FAR), 0)
    yield
    for half in (1, 0):
        for e in reversed(range(len(FAR))):
            far[half, e].wait_recv()
            go_near(half, e, FAR[e])
    yield
    for copy in near.values():
        copy.wait_recv()
    copies += list(near.values()) + list(far.values()) + [side]


def region_exchange(group, x_ref, out_ref, sems, copies):
    send_sem, recv_sem = sems
    begun = []
    for i, (half, step) in enumerate(ALL):
        target = group.block(half, step)
        begun.append(
            send(
                x_ref.at[:, target], out_ref.at[:, group.me], send_sem.at[i], recv_sem.at[i],
                "region", target,
            )
        )
    out_ref[:, group.me] = x_ref[:, group.me]
    yield
    for copy in begun:
        copy.wait_recv()
    copies += begun


def run(steps):
    while True:
        try:
            next(steps)
        except StopIteration as end:
            return end.value


def advance(steps):
    next(steps)


def mode_buffers(a, rows, width):
    return [pltpu.VMEM((OTHERS + 1, a, rows, width), f32), pltpu.VMEM((OTHERS, a, rows, width), f32)]


def region_buffers(a, rows, width):
    return [
        pltpu.VMEM((2, 4, 4, a, rows, width), f32),
        pltpu.VMEM((2, 3, a, rows, width), f32),
        pltpu.VMEM((a, rows, width), f32),
    ]


MODE_SEMS = [DMA((OTHERS + 1,)), DMA((OTHERS + 1,)), DMA((OTHERS,)), DMA((OTHERS,))]
REGION_SEMS = [DMA((2, 4, 4)), DMA((2, 4, 4)), DMA((2, 3)), DMA((2, 3)), DMA((1,)), DMA((1,))]
EXCHANGE_SEMS = [DMA((len(ALL),)), DMA((len(ALL),))]


def own_band_of(owner_ref):
    region = lax.axis_index("region")
    found = 0
    for band in range(REGIONS):
        found = found + jnp.where(owner_ref[band] == region, band, 0)
    return found


def touching_frame(scan_ref, own_band, region):
    firsts = [scan_ref[region * F_DEV + frame, 0] for frame in range(F_DEV)]
    columns = [scan_ref[region * F_DEV + frame, 1] for frame in range(F_DEV)]
    gaps = [own_band - first // BAND for first in firsts]
    covers = [jnp.logical_and(gap >= 0, gap <= 2) for gap in gaps]
    first = jnp.where(covers[0], firsts[0], firsts[1])
    column = jnp.where(covers[0], columns[0], columns[1])
    return first, column, jnp.logical_or(covers[0], covers[1])


def prepare(scan_ref, owner_ref, object_ref, packed, table, bits):
    share = lax.axis_index("mode")
    own_band = own_band_of(owner_ref)

    @pl.loop(0, REGIONS, unroll=8)
    def _(region):
        _, column, _ = touching_frame(scan_ref, own_band, region)
        for plane in range(2):
            rows = pltpu.roll(object_ref[plane, share], (WIDTH - column) % WIDTH, 1)
            packed[plane, region] = rows[:, :N]

    numbers = lax.broadcasted_iota(jnp.int32, (SHARE, N), 0) + share * SHARE
    for frame in range(F_DEV):
        first = scan_ref[lax.axis_index("region") * F_DEV + frame, 0]
        anchor = first // BAND
        homes = [owner_ref[anchor + k] for k in range(3)]
        outer = jnp.where(numbers >= first - anchor * BAND, homes[0], homes[2])
        inner = jnp.full((SHARE, N), homes[1], jnp.int32)
        odd = jnp.full((SHARE, N), anchor % 2, jnp.int32) == 1
        table[frame * 2] = jnp.where(odd, inner, outer)
        table[frame * 2 + 1] = jnp.where(odd, outer, inner)
        for k in range(TURNS):
            bits[frame * TURNS + k] = jnp.full((1, N), first // 2**k % 2, jnp.int32)


def select_rows(table, bands, plane, out_ref):
    share = lax.axis_index("mode")
    for k in range(2 * F_DEV):
        homes = table[k]
        rows = bands[plane, 0]
        for block in range(1, REGIONS):
            rows = jnp.where(homes == block, bands[plane, block], rows)
        out_ref[plane * 2 * F_DEV + k, share] = rows


def place_terms(table, terms, plane, out_ref):
    for block in range(REGIONS):
        rows = jnp.zeros((SHARE, N), f32)
        for k in range(2 * F_DEV):
            rows = jnp.where(table[k] == block, terms[k], rows)
        out_ref[plane, block] = rows


def turn_rows(values, bits, frame, back):
    for k in range(TURNS):
        here = jnp.broadcast_to(bits[frame * TURNS + k], (N, N)) == 1
        shift = N - 2**k if back else 2**k
        if shift % 8 == 0:
            rolled = [jnp.concatenate([v[N - shift:], v[:N - shift]], axis=0) for v in values]
        else:
            rolled = [pltpu.roll(v, shift, 0) for v in values]
        values = [jnp.where(here, r, v) for r, v in zip(rolled, values)]
    return values


def update_kernel(scan_ref, owner_ref, parts_ref, object_ref, power_ref, out_ref, tall, placed):
    share = lax.axis_index("mode")
    own_band = own_band_of(owner_ref)
    tall[0:BAND, :] = jnp.zeros((BAND, N), f32)
    tall[BAND:BAND + N, :] = power_ref[...]
    tall[BAND + N:, :] = jnp.zeros((BAND + SHARE, N), f32)
    placed[...] = jnp.zeros(placed.shape, f32)
    blank = jnp.zeros((SHARE, WIDTH - N), f32)

    @pl.loop(0, REGIONS, unroll=8)
    def _(region):
        first, column, covers = touching_frame(scan_ref, own_band, region)
        start = jnp.where(covers, BAND + own_band * BAND - first, 0) + share * SHARE
        base = pl.multiple_of(start // 8 * 8, 8)
        rows = pltpu.roll(tall[pl.ds(base, 2 * SHARE), :], (2 * SHARE - start % 8) % (2 * SHARE), 0)
        rows = jnp.where(covers, rows[:SHARE], 0.0)
        for k, part in enumerate((parts_ref[0, region], parts_ref[1, region], rows)):
            wide = pltpu.roll(jnp.concatenate([part, blank], axis=1), column, 1)
            placed[k] = placed[k] + wide

    scale = placed[2] + 1.0
    for plane in range(2):
        out_ref[plane] = object_ref[plane, share] + placed[plane] / scale


def gather_rows_kernel(x_ref, out_ref, *sems):
    group = ModeGroup()
    copies = []
    greet(group.peers())
    out_ref[:, group.me] = x_ref[...]
    run(mode_gather(group, out_ref, sems, copies))
    for copy in copies:
        copy.wait_send()


def split(x):
    high = x.astype(bf16)
    low = (x - high.astype(f32)).astype(bf16)
    return high, low


def transform(real, imag, tables, sign):
    ch, cl, sh, sl = tables
    cosine = jnp.concatenate([ch, ch, cl], axis=1)
    sine = jnp.concatenate([sh, sh, sl], axis=1)
    minus = -sine
    if sign < 0:
        left_real = jnp.concatenate([cosine, sine], axis=1)
        left_imag = jnp.concatenate([minus, cosine], axis=1)
    else:
        left_real = jnp.concatenate([cosine, minus], axis=1)
        left_imag = jnp.concatenate([sine, cosine], axis=1)
    rh, rl = split(real)
    ih, il = split(imag)
    stacked = jnp.concatenate([rh, rl, rh, ih, il, ih], axis=0)
    mid_real = jnp.dot(left_real, stacked, preferred_element_type=f32)
    mid_imag = jnp.dot(left_imag, stacked, preferred_element_type=f32)
    rh, rl = split(mid_real)
    ih, il = split(mid_imag)
    beside = jnp.concatenate([rh, rl, rh, ih, il, ih], axis=1)
    cosine = jnp.concatenate([ch, ch, cl], axis=0)
    sine = jnp.concatenate([sh, sh, sl], axis=0)
    minus = -sine
    if sign < 0:
        right_real = jnp.concatenate([cosine, sine], axis=0)
        right_imag = jnp.concatenate([minus, cosine], axis=0)
    else:
        right_real = jnp.concatenate([cosine, minus], axis=0)
        right_imag = jnp.concatenate([sine, cosine], axis=0)
    return (
        jnp.dot(beside, right_real, preferred_element_type=f32),
        jnp.dot(beside, right_imag, preferred_element_type=f32),
    )


def load_tables(tables_ref):
    return tuple(tables_ref[i] for i in range(4))


def blocks(value, count):
    return value.reshape(count, N // count, N)


def whole(ref, k):
    return ref[k].reshape(N, N)


def program(
    packed, table, bits, probe_ref, measured_ref, tables_ref, probe_out, arrived, mode_power,
    bands, turned, windows, waves, power, intensity, summed, gradient, terms, parts, *rest,
):
    rest = list(rest)

    def take(count):
        taken = rest[:count]
        del rest[:count]
        return taken

    mode = ModeGroup()
    region = RegionGroup()
    copies = []
    tables = load_tables(tables_ref)

    greet(mode.peers() + region.peers())
    exchanges = []
    for plane in range(2):
        part = (pl.ds(plane, 1),)
        exchanges.append(region_exchange(region, packed.at[part], bands.at[part], take(2), copies))
        advance(exchanges[plane])
    gathers = []
    for plane in range(2):
        run(exchanges[plane])
        select_rows(table, bands, plane, turned)
        part = (pl.ds(plane * 2 * F_DEV, 2 * F_DEV),)
        gathers.append(mode_gather(mode, turned.at[part], take(4), copies))
        advance(gathers[plane])
        advance(gathers[plane])
    run(gathers[0])
    run(gathers[1])
    total = jnp.zeros((N, N), f32)
    for frame in range(F_DEV):
        values = [turned[k:k + 2].reshape(N, N) for k in (frame * 2, (F_DEV + frame) * 2)]
        for plane, value in enumerate(turn_rows(values, bits, frame, True)):
            windows[frame, plane] = value
            total = total + value * value
    power[0] = blocks(total, REGIONS)
    power_steps = region_scatter(region, power, *take(3), take(6), copies)
    advance(power_steps)

    def forward(frame, pr, pi):
        wr, wi = windows[frame, 0], windows[frame, 1]
        real, imag = transform(pr * wr - pi * wi, pr * wi + pi * wr, tables, -1)
        waves[frame, 0] = real
        waves[frame, 1] = imag
        intensity[frame] = blocks(real * real + imag * imag, MODES)

    def change(frame):
        factor = jnp.sqrt(measured_ref[frame]) / jnp.sqrt(whole(summed, frame) + 0.1) - 1.0
        return transform(waves[frame, 0] * factor, waves[frame, 1] * factor, tables, 1)

    pr, pi = whole(probe_ref, 0), whole(probe_ref, 1)
    forward(0, pr, pi)
    forward(1, pr, pi)
    first_two = (pl.ds(0, F_DEV),)
    sums = mode_scatter(mode, intensity.at[first_two], *take(2), take(4), copies)
    advance(sums)
    advance(power_steps)
    total = run(sums)
    for frame in range(F_DEV):
        summed[frame, mode.me] = total[frame]
    gathers = mode_gather(mode, summed.at[first_two], take(4), copies)
    advance(gathers)
    advance(power_steps)
    run(gathers)
    power_total = run(power_steps)
    grad_real = jnp.zeros((N, N), f32)
    grad_imag = jnp.zeros((N, N), f32)
    for frame in range(F_DEV):
        cr, ci = change(frame)
        wr, wi = windows[frame, 0], windows[frame, 1]
        grad_real = grad_real + (wr * cr + wi * ci)
        grad_imag = grad_imag + (wr * ci - wi * cr)
    gradient[0] = blocks(grad_real, REGIONS)
    gradient[1] = blocks(grad_imag, REGIONS)
    total = run(region_scatter(region, gradient, *take(3), take(6), copies))
    probe_out[:, region.me] = probe_ref[:, region.me] + total / (power_total + 1.0)
    run(region_gather(region, probe_out, take(6), copies))

    pr, pi = whole(probe_out, 0), whole(probe_out, 1)
    strength, strength_sum = take(2)
    strength[0] = blocks(pr * pr + pi * pi, MODES)
    strengths = mode_scatter(mode, strength, *take(2), take(4), copies)
    strength_gathers = mode_gather(mode, strength_sum, take(4), copies)
    advance(strengths)
    intensity_again, summed_again = take(2)
    intensity = intensity_again
    summed = summed_again
    forward(0, pr, pi)
    forward(1, pr, pi)
    total = run(mode_scatter(mode, intensity, *take(2), take(4), copies))
    summed[:, mode.me] = total
    run(mode_gather(mode, summed, take(4), copies))
    for frame in range(F_DEV):
        cr, ci = change(frame)
        values = [pr * cr + pi * ci, pr * ci - pi * cr]
        for plane, value in enumerate(turn_rows(values, bits, frame, False)):
            k = (plane * F_DEV + frame) * 2
            terms[k:k + 2] = value.reshape(2, MODES, SHARE, N)
    scatters = []
    for plane in range(2):
        part = (pl.ds(plane * 2 * F_DEV, 2 * F_DEV),)
        scatters.append(mode_scatter(mode, terms.at[part], *take(2), take(4), copies))
        advance(scatters[plane])
    advance(scatters[0])
    advance(scatters[1])
    exchanges = []
    for plane in range(2):
        place_terms(table, run(scatters[plane]), plane, parts)
        part = (pl.ds(plane, 1),)
        exchanges.append(region_exchange(region, parts.at[part], arrived.at[part], take(2), copies))
        advance(exchanges[plane])
    advance(strengths)
    strength_sum[:, mode.me] = run(strengths)
    run(strength_gathers)
    mode_power[...] = whole(strength_sum, 0)
    run(exchanges[0])
    run(exchanges[1])
    for copy in copies:
        copy.wait_send()


def vmem(*shape):
    return pltpu.VMEM(shape, f32)


SCRATCH = [
    vmem(2, REGIONS, SHARE, N),
    vmem(8, MODES, SHARE, N),
    vmem(F_DEV, 2, N, N),
    vmem(F_DEV, 2, N, N),
    vmem(1, REGIONS, 8, N),
    vmem(F_DEV, MODES, 16, N),
    vmem(F_DEV, MODES, 16, N),
    vmem(2, REGIONS, 8, N),
    vmem(8, MODES, SHARE, N),
    vmem(2, REGIONS, SHARE, N),
    *EXCHANGE_SEMS, *EXCHANGE_SEMS,
    *MODE_SEMS, *MODE_SEMS,
    *region_buffers(1, 8, N), *REGION_SEMS,
    *mode_buffers(F_DEV, 16, N), *MODE_SEMS,
    *MODE_SEMS,
    *region_buffers(2, 8, N), *REGION_SEMS,
    *REGION_SEMS,
    vmem(1, MODES, 16, N), vmem(1, MODES, 16, N),
    *mode_buffers(1, 16, N), *MODE_SEMS,
    *MODE_SEMS,
    vmem(F_DEV, MODES, 16, N), vmem(F_DEV, MODES, 16, N),
    *mode_buffers(F_DEV, 16, N), *MODE_SEMS,
    *MODE_SEMS,
    *mode_buffers(2 * F_DEV, SHARE, N), *MODE_SEMS,
    *mode_buffers(2 * F_DEV, SHARE, N), *MODE_SEMS,
    *EXCHANGE_SEMS, *EXCHANGE_SEMS,
]


def call(kernel, name, outs, n_smem, args, scratch=(), collective_id=None):
    params = pltpu.CompilerParams(vmem_limit_bytes=60 * 2**20)
    if collective_id is not None:
        params = pltpu.CompilerParams(
            collective_id=collective_id, has_side_effects=True, vmem_limit_bytes=60 * 2**20
        )
    return pl.pallas_call(
        kernel,
        name=name,
        out_shape=[jax.ShapeDtypeStruct(*out) for out in outs],
        in_specs=[SMEM] * n_smem + [VMEM] * (len(args) - n_smem),
        out_specs=[VMEM] * len(outs),
        scratch_shapes=list(scratch),
        compiler_params=params,
    )(*args)


def body(measured, probe_modes, object_bands, scan_offsets, band_owner):
    shares = object_bands.reshape(2, MODES, SHARE, WIDTH)
    exchanged = ((2, REGIONS, SHARE, N), f32)
    packed, table, bits = call(
        prepare, "prepare",
        [exchanged, ((2 * F_DEV, SHARE, N), jnp.int32), ((F_DEV * TURNS, 1, N), jnp.int32)],
        2, [scan_offsets, band_owner, shares],
    )
    probe, arrived, power = call(
        program, "ptychography", [((2, REGIONS, 8, N), f32), exchanged, ((N, N), f32)], 0,
        [packed, table, bits, probe_modes.reshape(2, REGIONS, 8, N), measured, jnp.asarray(table_array())],
        SCRATCH, 1,
    )
    (rows,) = call(
        update_kernel, "update", [((2, SHARE, WIDTH), f32)], 2,
        [scan_offsets, band_owner, arrived, shares, power],
        [vmem(2 * BAND + N + SHARE, N), vmem(3, SHARE, WIDTH)],
    )
    (object_out,) = call(
        gather_rows_kernel, "gather_rows", [((2, MODES, SHARE, WIDTH), f32)], 0, [rows], MODE_SEMS, 2
    )
    return probe.reshape(2, 1, N, N), object_out.reshape(2, BAND, WIDTH)


def table_array():
    product = np.arange(N)[:, None] * np.arange(N)[None, :] % N
    angles = product * (2.0 * math.pi / N)
    pieces = []
    for values in (np.cos(angles) / 16.0, np.sin(angles) / 16.0):
        high = values.astype(bf16)
        pieces += [high, (values - high.astype(np.float64)).astype(bf16)]
    return np.stack(pieces)


def solution(mesh):
    in_specs = (
        P("region", None, None),
        P(None, "mode", None, None),
        P(None, "region", None),
        P(),
        P(),
    )
    out_specs = (P(None, "mode", None, None), P(None, "region", None))
    return jax.shard_map(body, mesh=mesh, in_specs=in_specs, out_specs=out_specs, check_vma=False)
```

```python
import functools
import math

import jax
import jax.numpy as jnp
import numpy as np
from jax import lax
from jax.experimental import pallas as pl
from jax.experimental.pallas import tpu as pltpu
from jax.sharding import PartitionSpec as P

N = 256
BAND = 128
WIDTH = 512
FRAMES = 64
F_DEV = 2
REGIONS = 32
MODES = 16
Z = 16
Y = 4
SHARE = BAND // MODES
TURNS = 8
f32 = jnp.float32
bf16 = jnp.bfloat16

VMEM = pl.BlockSpec(memory_space=pltpu.VMEM)
SMEM = pl.BlockSpec(memory_space=pltpu.SMEM)
DMA = pltpu.SemaphoreType.DMA

NEAR = ((2, 1), (2, 0), (1, 1), (3, 1), (1, 0), (3, 0), (0, 1), (0, 0))
OTHERS = len(NEAR) - 1


def send(src, dst, send_sem, recv_sem, axis, index):
    copy = pltpu.make_async_remote_copy(
        src_ref=src,
        dst_ref=dst,
        send_sem=send_sem,
        recv_sem=recv_sem,
        device_id={axis: index},
        device_id_type=pl.DeviceIdType.MESH,
    )
    copy.start()
    return copy


def greet(peers):
    barrier = pltpu.get_barrier_semaphore()
    for axis, peer in peers:
        pl.semaphore_signal(
            barrier, inc=1, device_id={axis: peer}, device_id_type=pl.DeviceIdType.MESH
        )
    pl.semaphore_wait(barrier, len(peers))


class ModeGroup:
    def __init__(self):
        self.me = lax.axis_index("mode")
        self.y = self.me // 4
        self.x = (self.me // 2) % 2
        self.core = self.me % 2
        self.twin = self.me + 1 - 2 * self.core

    def chip(self, dy, dx):
        return ((self.y + dy) % Y) * 2 + (self.x + dx) % 2

    def chip_before(self, dy, dx):
        return ((self.y + Y - dy) % Y) * 2 + (self.x + 2 - dx) % 2

    def peers(self):
        chips = [2 * self.chip(dy, dx) + self.core for dy, dx in NEAR[:OTHERS]]
        return [("mode", peer) for peer in chips + [self.twin]]


def mode_scatter(group, x_ref, twin_buf, peer_buf, sems, copies):
    twin_send, twin_recv, peer_send, peer_recv = sems
    twin_copies = []
    for i, (dy, dx) in enumerate(NEAR):
        block = 2 * group.chip(dy, dx) + 1 - group.core
        twin_copies.append(
            send(x_ref.at[:, block], twin_buf.at[i], twin_send.at[i], twin_recv.at[i], "mode", group.twin)
        )
    yield
    peer_copies = []
    for i, (dy, dx) in enumerate(NEAR):
        target = 2 * group.chip(dy, dx) + group.core
        twin_copies[i].wait_recv()
        twin_buf[i] = twin_buf[i] + x_ref[:, target]
        if i < OTHERS:
            peer_copies.append(
                send(twin_buf.at[i], peer_buf.at[i], peer_send.at[i], peer_recv.at[i], "mode", target)
            )
    yield
    total = twin_buf[OTHERS]
    for i in reversed(range(OTHERS)):
        peer_copies[i].wait_recv()
        total = total + peer_buf[i]
    copies += twin_copies + peer_copies
    return total


def mode_gather(group, out_ref, sems, copies):
    twin_send, twin_recv, peer_send, peer_recv = sems
    mine = out_ref.at[:, group.me]
    peer_copies = []
    for i, (dy, dx) in enumerate(NEAR[:OTHERS]):
        target = 2 * group.chip(dy, dx) + group.core
        peer_copies.append(send(mine, mine, peer_send.at[i], peer_recv.at[i], "mode", target))
    twin_copies = [
        send(mine, mine, twin_send.at[OTHERS], twin_recv.at[OTHERS], "mode", group.twin)
    ]
    yield
    for i in reversed(range(OTHERS)):
        dy, dx = NEAR[i]
        block = out_ref.at[:, 2 * group.chip_before(dy, dx) + group.core]
        peer_copies[i].wait_recv()
        twin_copies.append(send(block, block, twin_send.at[i], twin_recv.at[i], "mode", group.twin))
    yield
    for copy in twin_copies:
        copy.wait_recv()
    copies += twin_copies + peer_copies


class RegionGroup:
    def __init__(self):
        self.me = lax.axis_index("region")
        self.x = self.me // Z
        self.z = self.me % Z
        self.partner = (1 - self.x) * Z + self.z

    def at(self, step):
        return self.x * Z + (self.z + step % Z) % Z

    def block(self, half, step):
        side = self.x if half == 1 else 1 - self.x
        return side * Z + (self.z + step % Z) % Z

    def peers(self):
        return [("region", self.block(half, step)) for half, step in ALL]


FAR = (8, 4, 12)
NEXT = (1, -1, 2, -2)


ALL = tuple(
    (half, step)
    for step in (8, 7, 9, 6, 10, 5, 11, 4, 12, 3, 13, 2, 14, 1, 15, 0)
    for half in ((0, 1) if step else (0,))
)


def neighbours(step):
    return NEXT if step % 8 == 0 else NEXT[:2]


def region_scatter(group, x_ref, near_buf, far_buf, side_buf, sems, copies):
    near_send, near_recv, far_send, far_recv, side_send, side_recv = sems
    near = {}
    far = {}
    for half in (0, 1):
        for e, step in enumerate((*FAR, 0)):
            for t, turn in enumerate(neighbours(step)):
                near[half, e, t] = send(
                    x_ref.at[:, group.block(half, turn + step)], near_buf.at[half, e, t],
                    near_send.at[half, e, t], near_recv.at[half, e, t], "region", group.at(turn),
                )
    yield
    for half in (0, 1):
        for e, step in enumerate((*FAR, 0)):
            total = x_ref[:, group.block(half, step)]
            for t in range(len(neighbours(step))):
                near[half, e, t].wait_recv()
                total = total + near_buf[half, e, t]
            near_buf[half, e, 0] = total
            if step:
                far[half, e] = send(
                    near_buf.at[half, e, 0], far_buf.at[half, e], far_send.at[half, e],
                    far_recv.at[half, e], "region", group.block(half, step),
                )
            elif half == 0:
                side = send(
                    near_buf.at[half, e, 0], side_buf, side_send.at[0], side_recv.at[0],
                    "region", group.partner,
                )
    yield
    side.wait_recv()
    total = near_buf[1, len(FAR), 0] + side_buf[...]
    for e in reversed(range(len(FAR))):
        for half in (0, 1):
            far[half, e].wait_recv()
            total = total + far_buf[half, e]
    copies += list(near.values()) + list(far.values()) + [side]
    yield
    return total


def region_gather(group, out_ref, sems, copies):
    near_send, near_recv, far_send, far_recv, side_send, side_recv = sems
    near = {}
    far = {}
    mine = out_ref.at[:, group.me]
    side = send(mine, mine, side_send.at[0], side_recv.at[0], "region", group.partner)

    def go_near(half, e, step):
        block = out_ref.at[:, group.block(half, -step)]
        for t, turn in enumerate(neighbours(step)):
            near[half, e, t] = send(
                block, block, near_send.at[half, e, t], near_recv.at[half, e, t],
                "region", group.at(turn),
            )

    for e, step in enumerate(FAR):
        for half in (0, 1):
            far[half, e] = send(
                mine, mine, far_send.at[half, e], far_recv.at[half, e],
                "region", group.block(half, step),
            )
    go_near(1, len(FAR), 0)
    side.wait_recv()
    go_near(0, len(FAR), 0)
    yield
    for half in (1, 0):
        for e in reversed(range(len(FAR))):
            far[half, e].wait_recv()
            go_near(half, e, FAR[e])
    yield
    for copy in near.values():
        copy.wait_recv()
    copies += list(near.values()) + list(far.values()) + [side]


def region_exchange(group, x_ref, out_ref, sems, copies):
    send_sem, recv_sem = sems
    begun = []
    for i, (half, step) in enumerate(ALL):
        target = group.block(half, step)
        begun.append(
            send(
                x_ref.at[:, target], out_ref.at[:, group.me], send_sem.at[i], recv_sem.at[i],
                "region", target,
            )
        )
    out_ref[:, group.me] = x_ref[:, group.me]
    yield
    for copy in begun:
        copy.wait_recv()
    copies += begun


def run(steps):
    while True:
        try:
            next(steps)
        except StopIteration as end:
            return end.value


def advance(steps):
    next(steps)


def mode_buffers(a, rows, width):
    return [pltpu.VMEM((OTHERS + 1, a, rows, width), f32), pltpu.VMEM((OTHERS, a, rows, width), f32)]


def region_buffers(a, rows, width):
    return [
        pltpu.VMEM((2, 4, 4, a, rows, width), f32),
        pltpu.VMEM((2, 3, a, rows, width), f32),
        pltpu.VMEM((a, rows, width), f32),
    ]


MODE_SEMS = [DMA((OTHERS + 1,)), DMA((OTHERS + 1,)), DMA((OTHERS,)), DMA((OTHERS,))]
REGION_SEMS = [DMA((2, 4, 4)), DMA((2, 4, 4)), DMA((2, 3)), DMA((2, 3)), DMA((1,)), DMA((1,))]
EXCHANGE_SEMS = [DMA((len(ALL),)), DMA((len(ALL),))]


def own_band_of(owner_ref):
    region = lax.axis_index("region")
    found = 0
    for band in range(REGIONS):
        found = found + jnp.where(owner_ref[band] == region, band, 0)
    return found


def touching_frame(scan_ref, own_band, region):
    firsts = [scan_ref[region * F_DEV + frame, 0] for frame in range(F_DEV)]
    columns = [scan_ref[region * F_DEV + frame, 1] for frame in range(F_DEV)]
    gaps = [own_band - first // BAND for first in firsts]
    covers = [jnp.logical_and(gap >= 0, gap <= 2) for gap in gaps]
    first = jnp.where(covers[0], firsts[0], firsts[1])
    column = jnp.where(covers[0], columns[0], columns[1])
    return first, column, jnp.logical_or(covers[0], covers[1])


def prepare(scan_ref, owner_ref, object_ref, packed, table, bits):
    share = lax.axis_index("mode")
    own_band = own_band_of(owner_ref)

    @pl.loop(0, REGIONS, unroll=8)
    def _(region):
        _, column, _ = touching_frame(scan_ref, own_band, region)
        for plane in range(2):
            rows = pltpu.roll(object_ref[plane, share], (WIDTH - column) % WIDTH, 1)
            packed[plane, region] = rows[:, :N]

    numbers = lax.broadcasted_iota(jnp.int32, (SHARE, N), 0) + share * SHARE
    for frame in range(F_DEV):
        first = scan_ref[lax.axis_index("region") * F_DEV + frame, 0]
        anchor = first // BAND
        homes = [owner_ref[anchor + k] for k in range(3)]
        outer = jnp.where(numbers >= first - anchor * BAND, homes[0], homes[2])
        inner = jnp.full((SHARE, N), homes[1], jnp.int32)
        odd = jnp.full((SHARE, N), anchor % 2, jnp.int32) == 1
        table[frame * 2] = jnp.where(odd, inner, outer)
        table[frame * 2 + 1] = jnp.where(odd, outer, inner)
        for k in range(TURNS):
            bits[frame * TURNS + k] = jnp.full((1, N), first // 2**k % 2, jnp.int32)


def select_rows(table, bands, plane, out_ref):
    share = lax.axis_index("mode")
    for k in range(2 * F_DEV):
        homes = table[k]
        rows = bands[plane, 0]
        for block in range(1, REGIONS):
            rows = jnp.where(homes == block, bands[plane, block], rows)
        out_ref[plane * 2 * F_DEV + k, share] = rows


def place_terms(table, terms, plane, out_ref):
    for block in range(REGIONS):
        rows = jnp.zeros((SHARE, N), f32)
        for k in range(2 * F_DEV):
            rows = jnp.where(table[k] == block, terms[k], rows)
        out_ref[plane, block] = rows


def turn_rows(values, bits, frame, back):
    for k in range(TURNS):
        here = jnp.broadcast_to(bits[frame * TURNS + k], (N, N)) == 1
        shift = N - 2**k if back else 2**k
        if shift % 8 == 0:
            rolled = [jnp.concatenate([v[N - shift:], v[:N - shift]], axis=0) for v in values]
        else:
            rolled = [pltpu.roll(v, shift, 0) for v in values]
        values = [jnp.where(here, r, v) for r, v in zip(rolled, values)]
    return values


def update_kernel(scan_ref, owner_ref, parts_ref, object_ref, power_ref, out_ref, tall, placed):
    share = lax.axis_index("mode")
    own_band = own_band_of(owner_ref)
    tall[0:BAND, :] = jnp.zeros((BAND, N), f32)
    tall[BAND:BAND + N, :] = power_ref[...]
    tall[BAND + N:, :] = jnp.zeros((BAND + SHARE, N), f32)
    placed[...] = jnp.zeros(placed.shape, f32)
    blank = jnp.zeros((SHARE, WIDTH - N), f32)

    @pl.loop(0, REGIONS, unroll=8)
    def _(region):
        first, column, covers = touching_frame(scan_ref, own_band, region)
        start = jnp.where(covers, BAND + own_band * BAND - first, 0) + share * SHARE
        base = pl.multiple_of(start // 8 * 8, 8)
        rows = pltpu.roll(tall[pl.ds(base, 2 * SHARE), :], (2 * SHARE - start % 8) % (2 * SHARE), 0)
        rows = jnp.where(covers, rows[:SHARE], 0.0)
        for k, part in enumerate((parts_ref[0, region], parts_ref[1, region], rows)):
            wide = pltpu.roll(jnp.concatenate([part, blank], axis=1), column, 1)
            placed[k] = placed[k] + wide

    scale = placed[2] + 1.0
    for plane in range(2):
        out_ref[plane] = object_ref[plane, share] + placed[plane] / scale


def gather_rows_kernel(x_ref, out_ref, *sems):
    group = ModeGroup()
    copies = []
    greet(group.peers())
    out_ref[:, group.me] = x_ref[...]
    run(mode_gather(group, out_ref, sems, copies))
    for copy in copies:
        copy.wait_send()


def split(x):
    high = x.astype(bf16)
    low = (x - high.astype(f32)).astype(bf16)
    return high, low


def transform(real, imag, tables, sign):
    ch, cl, sh, sl = tables
    cosine = jnp.concatenate([ch, ch, cl], axis=1)
    sine = jnp.concatenate([sh, sh, sl], axis=1)
    minus = -sine
    if sign < 0:
        left_real = jnp.concatenate([cosine, sine], axis=1)
        left_imag = jnp.concatenate([minus, cosine], axis=1)
    else:
        left_real = jnp.concatenate([cosine, minus], axis=1)
        left_imag = jnp.concatenate([sine, cosine], axis=1)
    rh, rl = split(real)
    ih, il = split(imag)
    stacked = jnp.concatenate([rh, rl, rh, ih, il, ih], axis=0)
    mid_real = jnp.dot(left_real, stacked, preferred_element_type=f32)
    mid_imag = jnp.dot(left_imag, stacked, preferred_element_type=f32)
    rh, rl = split(mid_real)
    ih, il = split(mid_imag)
    beside = jnp.concatenate([rh, rl, rh, ih, il, ih], axis=1)
    cosine = jnp.concatenate([ch, ch, cl], axis=0)
    sine = jnp.concatenate([sh, sh, sl], axis=0)
    minus = -sine
    if sign < 0:
        right_real = jnp.concatenate([cosine, sine], axis=0)
        right_imag = jnp.concatenate([minus, cosine], axis=0)
    else:
        right_real = jnp.concatenate([cosine, minus], axis=0)
        right_imag = jnp.concatenate([sine, cosine], axis=0)
    return (
        jnp.dot(beside, right_real, preferred_element_type=f32),
        jnp.dot(beside, right_imag, preferred_element_type=f32),
    )


def load_tables(tables_ref):
    return tuple(tables_ref[i] for i in range(4))


def blocks(value, count):
    return value.reshape(count, N // count, N)


def whole(ref, k):
    return ref[k].reshape(N, N)


def program(
    packed, table, bits, probe_ref, measured_ref, tables_ref, probe_out, arrived, mode_power,
    bands, turned, windows, waves, power, intensity, summed, gradient, terms, parts, *rest,
):
    rest = list(rest)

    def take(count):
        taken = rest[:count]
        del rest[:count]
        return taken

    mode = ModeGroup()
    region = RegionGroup()
    copies = []
    tables = load_tables(tables_ref)

    greet(mode.peers() + region.peers())
    exchanges = []
    for plane in range(2):
        part = (pl.ds(plane, 1),)
        exchanges.append(region_exchange(region, packed.at[part], bands.at[part], take(2), copies))
        advance(exchanges[plane])
    gathers = []
    for plane in range(2):
        run(exchanges[plane])
        select_rows(table, bands, plane, turned)
        part = (pl.ds(plane * 2 * F_DEV, 2 * F_DEV),)
        gathers.append(mode_gather(mode, turned.at[part], take(4), copies))
        advance(gathers[plane])
        advance(gathers[plane])
    run(gathers[0])
    run(gathers[1])
    total = jnp.zeros((N, N), f32)
    for frame in range(F_DEV):
        values = [turned[k:k + 2].reshape(N, N) for k in (frame * 2, (F_DEV + frame) * 2)]
        for plane, value in enumerate(turn_rows(values, bits, frame, True)):
            windows[frame, plane] = value
            total = total + value * value
    power[0] = blocks(total, REGIONS)
    power_steps = region_scatter(region, power, *take(3), take(6), copies)
    advance(power_steps)

    def forward(frame, pr, pi):
        wr, wi = windows[frame, 0], windows[frame, 1]
        real, imag = transform(pr * wr - pi * wi, pr * wi + pi * wr, tables, -1)
        waves[frame, 0] = real
        waves[frame, 1] = imag
        intensity[frame] = blocks(real * real + imag * imag, MODES)

    def change(frame):
        factor = jnp.sqrt(measured_ref[frame]) / jnp.sqrt(whole(summed, frame) + 0.1) - 1.0
        return transform(waves[frame, 0] * factor, waves[frame, 1] * factor, tables, 1)

    pr, pi = whole(probe_ref, 0), whole(probe_ref, 1)
    forward(0, pr, pi)
    forward(1, pr, pi)
    first_two = (pl.ds(0, F_DEV),)
    sums = mode_scatter(mode, intensity.at[first_two], *take(2), take(4), copies)
    advance(sums)
    advance(power_steps)
    total = run(sums)
    for frame in range(F_DEV):
        summed[frame, mode.me] = total[frame]
    gathers = mode_gather(mode, summed.at[first_two], take(4), copies)
    advance(gathers)
    advance(power_steps)
    run(gathers)
    power_total = run(power_steps)
    grad_real = jnp.zeros((N, N), f32)
    grad_imag = jnp.zeros((N, N), f32)
    for frame in range(F_DEV):
        cr, ci = change(frame)
        wr, wi = windows[frame, 0], windows[frame, 1]
        grad_real = grad_real + (wr * cr + wi * ci)
        grad_imag = grad_imag + (wr * ci - wi * cr)
    gradient[0] = blocks(grad_real, REGIONS)
    gradient[1] = blocks(grad_imag, REGIONS)
    total = run(region_scatter(region, gradient, *take(3), take(6), copies))
    probe_out[:, region.me] = probe_ref[:, region.me] + total / (power_total + 1.0)
    run(region_gather(region, probe_out, take(6), copies))

    pr, pi = whole(probe_out, 0), whole(probe_out, 1)
    strength, strength_sum = take(2)
    strength[0] = blocks(pr * pr + pi * pi, MODES)
    strengths = mode_scatter(mode, strength, *take(2), take(4), copies)
    strength_gathers = mode_gather(mode, strength_sum, take(4), copies)
    advance(strengths)
    intensity_again, summed_again = take(2)
    intensity = intensity_again
    summed = summed_again
    forward(0, pr, pi)
    forward(1, pr, pi)
    total = run(mode_scatter(mode, intensity, *take(2), take(4), copies))
    summed[:, mode.me] = total
    run(mode_gather(mode, summed, take(4), copies))
    for frame in range(F_DEV):
        cr, ci = change(frame)
        values = [pr * cr + pi * ci, pr * ci - pi * cr]
        for plane, value in enumerate(turn_rows(values, bits, frame, False)):
            k = (plane * F_DEV + frame) * 2
            terms[k:k + 2] = value.reshape(2, MODES, SHARE, N)
    scatters = []
    for plane in range(2):
        part = (pl.ds(plane * 2 * F_DEV, 2 * F_DEV),)
        scatters.append(mode_scatter(mode, terms.at[part], *take(2), take(4), copies))
        advance(scatters[plane])
    advance(scatters[0])
    advance(scatters[1])
    exchanges = []
    for plane in range(2):
        place_terms(table, run(scatters[plane]), plane, parts)
        part = (pl.ds(plane, 1),)
        exchanges.append(region_exchange(region, parts.at[part], arrived.at[part], take(2), copies))
        advance(exchanges[plane])
    advance(strengths)
    strength_sum[:, mode.me] = run(strengths)
    run(strength_gathers)
    mode_power[...] = whole(strength_sum, 0)
    run(exchanges[0])
    run(exchanges[1])
    for copy in copies:
        copy.wait_send()


def vmem(*shape):
    return pltpu.VMEM(shape, f32)


SCRATCH = [
    vmem(2, REGIONS, SHARE, N),
    vmem(8, MODES, SHARE, N),
    vmem(F_DEV, 2, N, N),
    vmem(F_DEV, 2, N, N),
    vmem(1, REGIONS, 8, N),
    vmem(F_DEV, MODES, 16, N),
    vmem(F_DEV, MODES, 16, N),
    vmem(2, REGIONS, 8, N),
    vmem(8, MODES, SHARE, N),
    vmem(2, REGIONS, SHARE, N),
    *EXCHANGE_SEMS, *EXCHANGE_SEMS,
    *MODE_SEMS, *MODE_SEMS,
    *region_buffers(1, 8, N), *REGION_SEMS,
    *mode_buffers(F_DEV, 16, N), *MODE_SEMS,
    *MODE_SEMS,
    *region_buffers(2, 8, N), *REGION_SEMS,
    *REGION_SEMS,
    vmem(1, MODES, 16, N), vmem(1, MODES, 16, N),
    *mode_buffers(1, 16, N), *MODE_SEMS,
    *MODE_SEMS,
    vmem(F_DEV, MODES, 16, N), vmem(F_DEV, MODES, 16, N),
    *mode_buffers(F_DEV, 16, N), *MODE_SEMS,
    *MODE_SEMS,
    *mode_buffers(2 * F_DEV, SHARE, N), *MODE_SEMS,
    *mode_buffers(2 * F_DEV, SHARE, N), *MODE_SEMS,
    *EXCHANGE_SEMS, *EXCHANGE_SEMS,
]


def call(kernel, name, outs, n_smem, args, scratch=(), collective_id=None):
    params = pltpu.CompilerParams(vmem_limit_bytes=60 * 2**20)
    if collective_id is not None:
        params = pltpu.CompilerParams(
            collective_id=collective_id, has_side_effects=True, vmem_limit_bytes=60 * 2**20
        )
    return pl.pallas_call(
        kernel,
        name=name,
        out_shape=[jax.ShapeDtypeStruct(*out) for out in outs],
        in_specs=[SMEM] * n_smem + [VMEM] * (len(args) - n_smem),
        out_specs=[VMEM] * len(outs),
        scratch_shapes=list(scratch),
        compiler_params=params,
    )(*args)


def body(measured, probe_modes, object_bands, scan_offsets, band_owner):
    shares = object_bands.reshape(2, MODES, SHARE, WIDTH)
    exchanged = ((2, REGIONS, SHARE, N), f32)
    packed, table, bits = call(
        prepare, "prepare",
        [exchanged, ((2 * F_DEV, SHARE, N), jnp.int32), ((F_DEV * TURNS, 1, N), jnp.int32)],
        2, [scan_offsets, band_owner, shares],
    )
    probe, arrived, power = call(
        program, "ptychography", [((2, REGIONS, 8, N), f32), exchanged, ((N, N), f32)], 0,
        [packed, table, bits, probe_modes.reshape(2, REGIONS, 8, N), measured, jnp.asarray(table_array())],
        SCRATCH, 1,
    )
    (rows,) = call(
        update_kernel, "update", [((2, SHARE, WIDTH), f32)], 2,
        [scan_offsets, band_owner, arrived, shares, power],
        [vmem(2 * BAND + N + SHARE, N), vmem(3, SHARE, WIDTH)],
    )
    (object_out,) = call(
        gather_rows_kernel, "gather_rows", [((2, MODES, SHARE, WIDTH), f32)], 0, [rows], MODE_SEMS, 2
    )
    return probe.reshape(2, 1, N, N), object_out.reshape(2, BAND, WIDTH)


def table_array():
    product = np.arange(N)[:, None] * np.arange(N)[None, :] % N
    angles = product * (2.0 * math.pi / N)
    pieces = []
    for values in (np.cos(angles) / 16.0, np.sin(angles) / 16.0):
        high = values.astype(bf16)
        pieces += [high, (values - high.astype(np.float64)).astype(bf16)]
    return np.stack(pieces)


def solution(mesh):
    in_specs = (
        P("region", None, None),
        P(None, "mode", None, None),
        P(None, "region", None),
        P(),
        P(),
    )
    out_specs = (P(None, "mode", None, None), P(None, "region", None))
    return jax.shard_map(body, mesh=mesh, in_specs=in_specs, out_specs=out_specs, check_vma=False)
```
